32 devices in a mesh: dp: 4 (over y, x), wide: 8 (over z, core).
Axes of the slice: x: 2, y: 2, z: 4, core: 2. Of those that a mesh axis runs over, the one named last changes fastest.
Arguments:
- tokens: bfloat16 [49152, 768], P(('dp', 'wide')), may hold values from -6 to 6
- cotangent: bfloat16 [49152, 768], P(('dp', 'wide')), may hold values from -6 to 6
- valid_token_length: int32 [224], P(('dp', 'wide')), may hold values from 1 to 512, as said below
- query_weight_matrix: bfloat16 [768, 768], replicated, may hold values from -0.21875 to 0.21875
- key_weight_matrix: bfloat16 [768, 768], replicated, may hold values from -0.21875 to 0.21875
- value_weight_matrix: bfloat16 [768, 768], replicated, may hold values from -0.21875 to 0.21875
- attention_output_weight: bfloat16 [768, 768], replicated, may hold values from -0.875 to 0.875
- inner_ffn_weight: bfloat16 [768, 3072], replicated, may hold values from -0.21875 to 0.21875
- outer_ffn_weight: bfloat16 [3072, 768], replicated, may hold values from -0.109375 to 0.109375
- query_bias_vector: float32 [768], replicated, may hold values from -1.8 to 1.8
- value_bias_vector: float32 [768], replicated, may hold values from -1.8 to 1.8
- attention_output_bias: float32 [768], replicated, may hold values from -1.8 to 1.8
- hidden_ffn_bias: float32 [3072], replicated, may hold values from -1.8 to 1.8
- ffn_output_bias: float32 [768], replicated, may hold values from -1.8 to 1.8
- layer_norm_gains: float32 [2, 768], replicated, may hold values from 0.5 to 1.5
- layer_norm_biases: float32 [2, 768], replicated, may hold values from -1.8 to 1.8
- adapter_down_factors: float32 [2, 768, 8], replicated, may hold values from -0.21875 to 0.21875
- adapter_up_factors: float32 [2, 8, 768], replicated, may hold values from -0.3 to 0.3
- first_moment_estimate: float32 [24576], P('wide'), may hold values from -0.0005412659 to 0.0005412659
- second_moment_estimate: float32 [24576], P('wide'), may hold values from 4.0690104e-10 to 4.0690105e-09
- first_decay_factor: float32 [1], replicated, may hold values from 0.85 to 0.95
- second_decay_factor: float32 [1], replicated, may hold values from 0.998 to 0.9995
- optimizer_step_number: int32 [1], replicated, may hold values from 1 to 1024
Outputs:
- mixed: bfloat16 [49152, 768], P(('dp', 'wide'))
- input_token_gradient: bfloat16 [49152, 768], P(('dp', 'wide'))
- updated_down_factors: float32 [2, 768, 8], replicated
- updated_up_factors: float32 [2, 8, 768], replicated
- updated_first_moment: float32 [24576], P('wide')
- updated_second_moment: float32 [24576], P('wide')
The draws below stay inside these ranges and needn't reach their ends.
Inputs may be any that keep to these rules, and one draw needn't show every extreme that they name: `valid_token_length`: entry n * 7 + s belongs to sequence s of device n (dp slowest); sequences 0 to 3 of a device have 128 slots, the next 2 have 256, the last 1 have 512; every entry is at most its sequence's slots.
All inputs are finite; a program needn't handle non-finite values.
Results may differ from the reference program's by a relative error of at most 0.035.
Values sent between devices are 32-bit elements; how exact they have to be, the bound alone decides.
No kernel may reach another device: no remote copies, remote signals or barrier semaphores. Data moves between devices by JAX's collectives and lax.ppermute only.
A program may use at most 192 MiB of HBM per device.

```python
import math
import jax
import jax.numpy as jnp
from jax import lax

MODEL_DIMENSION = 768
HEADS = 12
HEAD_DIM = 64
FF = 3072
ADAPTER_RANK = 8
LEN_A = 128
LEN_B = 256
LEN_C = 512
BUCKET_TOK = 512
TOK_DEV = 1536
SEQ_DEV = 7
TOKEN_SLOTS = 49152
SEQS = 224
ADAPTER_ENTRIES = 24576
N_DP = 4
N_WIDE = 8


def draw_valid_token_length(key, part):
    seq_index = jnp.arange(SEQS, dtype=jnp.int32)
    device = seq_index // SEQ_DEV
    within = seq_index % SEQ_DEV
    first_end = BUCKET_TOK // LEN_A
    second_end = first_end + BUCKET_TOK // LEN_B
    length = jnp.where(within < first_end, LEN_A, jnp.where(within < second_end, LEN_B, LEN_C)).astype(jnp.int32)
    devices = SEQS // SEQ_DEV
    most_pad = (length - length // 8 - 1) * (devices - 1 - device) // (devices - 1)
    raw_draws = jax.random.randint(key, (SEQS,), 0, 1 << 20, dtype=jnp.int32)
    padding = most_pad // 2 + raw_draws % (most_pad - most_pad // 2 + 1)
    return (length - padding).astype(jnp.int32)


def block_levels(key, shape, shards, least, high):
    factor_of, own = 1.0, jax.random.fold_in(key, 6)
    for dim, shards_of in shards:
        steps = jnp.exp(jax.random.uniform(jax.random.fold_in(own, dim), (shards_of,), jnp.float32, least / len(shards), high / len(shards)))
        factor_of = factor_of * jnp.repeat(steps, shape[dim] // shards_of).reshape([-1 if axis == dim else 1 for axis in range(len(shape))])
    return factor_of


def bell_draw(key, extent, deviation, reach, cuts=(), kind=jnp.bfloat16):
    level = block_levels(key, extent, cuts, -0.22, 0.18) if cuts else 1.0
    drawn = jax.random.normal(key, extent, jnp.float32) * deviation * level
    return jnp.minimum(jnp.maximum(drawn, -reach), reach).astype(kind)


def setup_inputs(seed: int = 0) -> dict:
    key_list = jax.random.split(jax.random.key(seed), 24)
    tokens = bell_draw(key_list[0], (TOKEN_SLOTS, MODEL_DIMENSION), 1.0, 6.0, ((0, 32),))
    cotangent = bell_draw(key_list[1], (TOKEN_SLOTS, MODEL_DIMENSION), 1.0, 6.0, ((0, 32),))
    valid_token_length = draw_valid_token_length(jax.random.fold_in(key_list[23], 71), 0)
    query_weight_matrix = bell_draw(key_list[3], (MODEL_DIMENSION, MODEL_DIMENSION), MODEL_DIMENSION ** -0.5, 0.21875)
    key_weight_matrix = bell_draw(key_list[4], (MODEL_DIMENSION, MODEL_DIMENSION), MODEL_DIMENSION ** -0.5, 0.21875)
    value_weight_matrix = bell_draw(key_list[5], (MODEL_DIMENSION, MODEL_DIMENSION), MODEL_DIMENSION ** -0.5, 0.21875)
    attention_output_weight = bell_draw(key_list[6], (MODEL_DIMENSION, MODEL_DIMENSION), (MODEL_DIMENSION // 16) ** -0.5, 0.875)
    inner_ffn_weight = bell_draw(key_list[7], (MODEL_DIMENSION, FF), MODEL_DIMENSION ** -0.5, 0.21875)
    outer_ffn_weight = bell_draw(key_list[8], (FF, MODEL_DIMENSION), FF ** -0.5, 0.109375)
    query_bias_vector = bell_draw(key_list[9], (MODEL_DIMENSION,), 0.3, 1.8, (), jnp.float32)
    value_bias_vector = bell_draw(key_list[10], (MODEL_DIMENSION,), 0.3, 1.8, (), jnp.float32)
    attention_output_bias = bell_draw(key_list[11], (MODEL_DIMENSION,), 0.3, 1.8, (), jnp.float32)
    hidden_ffn_bias = bell_draw(key_list[12], (FF,), 0.3, 1.8, (), jnp.float32)
    ffn_output_bias = bell_draw(key_list[13], (MODEL_DIMENSION,), 0.3, 1.8, (), jnp.float32)
    layer_norm_gains = jnp.clip(1.0 + 0.1 * jax.random.normal(key_list[14], (2, MODEL_DIMENSION), jnp.float32), 0.5, 1.5)
    layer_norm_biases = bell_draw(key_list[15], (2, MODEL_DIMENSION), 0.3, 1.8, (), jnp.float32)
    adapter_down_factors = bell_draw(key_list[16], (2, MODEL_DIMENSION, ADAPTER_RANK), MODEL_DIMENSION ** -0.5, 0.21875, (), jnp.float32)
    adapter_up_factors = bell_draw(key_list[17], (2, ADAPTER_RANK, MODEL_DIMENSION), 0.05, 0.3, (), jnp.float32)
    first_moment_estimate = bell_draw(key_list[18], (ADAPTER_ENTRIES,), (0.02 / TOKEN_SLOTS ** 0.5), 0.0005412659, ((0, 8),), jnp.float32)
    second_moment_estimate = jnp.clip(jnp.exp(math.log(4.069010461904554e-09) - 2.3025851 * jax.random.uniform(key_list[19], (ADAPTER_ENTRIES,), jnp.float32) ** block_levels(key_list[19], (ADAPTER_ENTRIES,), ((0, 8),), -0.2, 0.2)), 4.069010406393403e-10, 4.069010461904554e-09)
    first_decay_factor = jnp.clip(jax.random.uniform(key_list[20], (1,), jnp.float32, 0.85, 0.95), 0.85, 0.95)
    second_decay_factor = jnp.clip(jax.random.uniform(key_list[21], (1,), jnp.float32, 0.998, 0.9995), 0.998, 0.9995)
    optimizer_step_number = jax.random.randint(key_list[22], (1,), 1, 1025).astype(jnp.int32)
    return dict(tokens=tokens, cotangent=cotangent, valid_token_length=valid_token_length, query_weight_matrix=query_weight_matrix, key_weight_matrix=key_weight_matrix, value_weight_matrix=value_weight_matrix, attention_output_weight=attention_output_weight, inner_ffn_weight=inner_ffn_weight, outer_ffn_weight=outer_ffn_weight, query_bias_vector=query_bias_vector, value_bias_vector=value_bias_vector, attention_output_bias=attention_output_bias, hidden_ffn_bias=hidden_ffn_bias, ffn_output_bias=ffn_output_bias, layer_norm_gains=layer_norm_gains, layer_norm_biases=layer_norm_biases, adapter_down_factors=adapter_down_factors, adapter_up_factors=adapter_up_factors, first_moment_estimate=first_moment_estimate, second_moment_estimate=second_moment_estimate, first_decay_factor=first_decay_factor, second_decay_factor=second_decay_factor, optimizer_step_number=optimizer_step_number)


@jax.custom_vjp
def reduced_precision(v):
    return lax.optimization_barrier(v.astype(jnp.bfloat16)).astype(jnp.float32)

@jax.custom_vjp
def reduced_precision_backward(v):
    return v

def low_keep(v):
    return (reduced_precision(v), None)

def low_pass(kept, grad):
    return (grad,)

def back_keep(v):
    return (v, None)

def back_low(kept, grad):
    return (reduced_precision(grad),)
reduced_precision.defvjp(low_keep, low_pass)
reduced_precision_backward.defvjp(back_keep, back_low)
highest = lax.Precision.HIGHEST
adapter_scale = 2.0
rate_first = 0.005
rate_second = 0.08
decay_first = 0.05
decay_second = 0.01
neg_large = -1e+30
norm_eps = 1e-05
adam_eps = 1e-08

def matrix_product(left, right):
    return jnp.dot(left, right, precision=highest, preferred_element_type=jnp.float32)

def layer_norm(values, gain, shift):
    centered = values - lax.optimization_barrier(jnp.mean(values, axis=-1, keepdims=True))
    variance = lax.optimization_barrier(jnp.mean(centered * centered, axis=-1, keepdims=True))
    return centered * lax.rsqrt(variance + norm_eps) * gain + shift

def exact_gelu(values):
    return jax.nn.gelu(values, approximate=False)

def bucket_masks(valid):
    mask_list = []
    offset_seq = 0
    for length in (LEN_A, LEN_B, LEN_C):
        count_seq = BUCKET_TOK // length
        seq_lens = valid[offset_seq:offset_seq + count_seq].reshape(BUCKET_TOK // LEN_C, LEN_C // length)
        offset_seq += count_seq
        positions = jnp.arange(length, dtype=jnp.int32)
        mask_list.append(positions[None, None, :] < seq_lens[:, :, None])
    return mask_list

def attend_group(packed):
    query_g, key_g, value_g, key_mask = packed
    score_scale = HEAD_DIM ** (-0.5)
    raw_scores = jnp.einsum('gqhd,gkhd->ghqk', query_g, key_g, precision=highest) * score_scale
    scores = jnp.where(key_mask[:, None, None, :], reduced_precision_backward(raw_scores), neg_large)
    row_top = lax.optimization_barrier(jnp.max(scores, axis=-1, keepdims=True))
    exponent = jnp.exp(scores - row_top)
    attn_probs = exponent / lax.optimization_barrier(jnp.sum(exponent, axis=-1, keepdims=True))
    return jnp.einsum('ghqk,gkhd->gqhd', reduced_precision(attn_probs), value_g, precision=highest)

def attention(query_rows, key_proj, value_projected, mask_list):
    checked = jax.checkpoint(attend_group)
    contexts = []
    for bucket_index, length in enumerate((LEN_A, LEN_B, LEN_C)):
        start_row = bucket_index * BUCKET_TOK
        end_row = start_row + BUCKET_TOK
        shape_g = (BUCKET_TOK // LEN_C, LEN_C // length, length, HEADS, HEAD_DIM)
        context_g = lax.map(checked, (query_rows[start_row:end_row].reshape(shape_g), key_proj[start_row:end_row].reshape(shape_g), value_projected[start_row:end_row].reshape(shape_g), mask_list[bucket_index]))
        contexts.append(context_g.reshape(BUCKET_TOK, MODEL_DIMENSION))
    return jnp.concatenate(contexts, axis=0)

def forward(tokens_function, down_factor_matrix, up_factor_matrix, mask_list, weights):
    query_weight_matrix, key_weight_matrix, value_weight_matrix, attention_output_weight, inner_ffn_weight, outer_ffn_weight, query_bias_vector, value_bias_vector, attention_output_bias, hidden_ffn_bias, ffn_output_bias, layer_norm_gains, layer_norm_biases = weights
    rounded_a = reduced_precision(down_factor_matrix)
    rounded_up_factor = reduced_precision(up_factor_matrix)
    query_down_projected = reduced_precision(reduced_precision_backward(matrix_product(tokens_function, rounded_a[0])))
    value_down_projected = reduced_precision(reduced_precision_backward(matrix_product(tokens_function, rounded_a[1])))
    query_rows = reduced_precision(reduced_precision_backward(matrix_product(tokens_function, query_weight_matrix) + query_bias_vector + adapter_scale * matrix_product(query_down_projected, rounded_up_factor[0])))
    key_proj = reduced_precision(reduced_precision_backward(matrix_product(tokens_function, key_weight_matrix)))
    value_projected = reduced_precision(reduced_precision_backward(matrix_product(tokens_function, value_weight_matrix) + value_bias_vector + adapter_scale * matrix_product(value_down_projected, rounded_up_factor[1])))
    context = reduced_precision(reduced_precision_backward(attention(query_rows, key_proj, value_projected, mask_list)))
    attn_out = reduced_precision_backward(matrix_product(context, attention_output_weight) + attention_output_bias)
    normed = layer_norm(attn_out + tokens_function, layer_norm_gains[0], layer_norm_biases[0])
    inner_pre = reduced_precision_backward(matrix_product(reduced_precision(normed), inner_ffn_weight) + hidden_ffn_bias)
    activation = reduced_precision(reduced_precision_backward(exact_gelu(inner_pre)))
    outer_out = reduced_precision_backward(matrix_product(activation, outer_ffn_weight) + ffn_output_bias)
    return layer_norm(outer_out + normed, layer_norm_gains[1], layer_norm_biases[1])

def adam_update(parameter_tree, gradient, first_state, second_state, beta_one, beta_two, step_count, step_rate, decay_rate):
    updated_first_moment = beta_one * first_state + (1.0 - beta_one) * gradient
    updated_second_moment = beta_two * second_state + (1.0 - beta_two) * gradient * gradient
    first_hat = updated_first_moment / (1.0 - jnp.power(beta_one, step_count))
    second_hat = updated_second_moment / (1.0 - jnp.power(beta_two, step_count))
    updated_parameters = parameter_tree * (1.0 - step_rate * decay_rate) - step_rate * first_hat / (jnp.sqrt(second_hat) + adam_eps)
    return (updated_parameters, updated_first_moment, updated_second_moment)

def reference(tokens, cotangent, valid_token_length, query_weight_matrix, key_weight_matrix, value_weight_matrix, attention_output_weight, inner_ffn_weight, outer_ffn_weight, query_bias_vector, value_bias_vector, attention_output_bias, hidden_ffn_bias, ffn_output_bias, layer_norm_gains, layer_norm_biases, adapter_down_factors, adapter_up_factors, first_moment_estimate, second_moment_estimate, first_decay_factor, second_decay_factor, optimizer_step_number):
    weights = (query_weight_matrix.astype(jnp.float32), key_weight_matrix.astype(jnp.float32), value_weight_matrix.astype(jnp.float32), attention_output_weight.astype(jnp.float32), inner_ffn_weight.astype(jnp.float32), outer_ffn_weight.astype(jnp.float32), query_bias_vector, value_bias_vector, attention_output_bias, hidden_ffn_bias, ffn_output_bias, layer_norm_gains, layer_norm_biases)
    blocks = N_DP * N_WIDE
    token_blocks = tokens.reshape(blocks, TOK_DEV, MODEL_DIMENSION)
    cot_blocks = cotangent.reshape(blocks, TOK_DEV, MODEL_DIMENSION)
    valid_blocks = valid_token_length.reshape(blocks, SEQ_DEV)

    def visit(carry, packed):
        token_block_rows, cot_block, valid_block = packed
        mask_list = bucket_masks(valid_block)
        row_valid = jnp.concatenate([mask_item.reshape(-1) for mask_item in mask_list]).astype(jnp.float32)

        def encoder_layer(tokens_function, down_factor_matrix, up_factor_matrix):
            return forward(tokens_function, down_factor_matrix, up_factor_matrix, mask_list, weights)
        mixed_precision_function, backward_function = jax.vjp(encoder_layer, token_block_rows.astype(jnp.float32), adapter_down_factors, adapter_up_factors)
        token_grad, grad_a, up_factor_gradient = backward_function(cot_block.astype(jnp.float32) * row_valid[:, None])
        return ((carry[0] + grad_a, carry[1] + up_factor_gradient), (mixed_precision_function.astype(jnp.bfloat16), token_grad.astype(jnp.bfloat16)))
    initial_sums = (jnp.zeros(adapter_down_factors.shape, jnp.float32), jnp.zeros(adapter_up_factors.shape, jnp.float32))
    (sum_a, sum_b), (mixed_precision_blocks, gradient_block_list) = lax.scan(visit, initial_sums, (token_blocks, cot_blocks, valid_blocks))
    count_all = jnp.sum(valid_token_length).astype(jnp.float32)
    gradient = jnp.concatenate([sum_a.reshape(-1), sum_b.reshape(-1)]) / count_all
    parameter_tree = jnp.concatenate([adapter_down_factors.reshape(-1), adapter_up_factors.reshape(-1)])
    inside_first_owner = jnp.arange(ADAPTER_ENTRIES, dtype=jnp.int32) < adapter_down_factors.size
    step_rate = jnp.where(inside_first_owner, rate_first, rate_second)
    decay_rate = jnp.where(inside_first_owner, decay_first, decay_second)
    updated_parameters, updated_first_moment, updated_second_moment = adam_update(parameter_tree, gradient, first_moment_estimate, second_moment_estimate, first_decay_factor[0], second_decay_factor[0], optimizer_step_number[0].astype(jnp.float32), step_rate, decay_rate)
    updated_down_factors = updated_parameters[:adapter_down_factors.size].reshape(adapter_down_factors.shape)
    updated_up_factors = updated_parameters[adapter_down_factors.size:].reshape(adapter_up_factors.shape)
    return (mixed_precision_blocks.reshape(TOKEN_SLOTS, MODEL_DIMENSION), gradient_block_list.reshape(TOKEN_SLOTS, MODEL_DIMENSION), updated_down_factors, updated_up_factors, updated_first_moment, updated_second_moment)
```

```python
import jax
import jax.numpy as jnp
from jax import lax
from jax.experimental import pallas as pl
from jax.experimental.pallas import tpu as pltpu
from jax.sharding import PartitionSpec as P

HEADS = 12
HEAD_DIM = 64
LEN_A = 128
LEN_B = 256
LEN_C = 512
BUCKET = 512
LANES = 128

adapter_scale = 2.0
rate_first = 0.005
rate_second = 0.08
decay_first = 0.05
decay_second = 0.01
neg_large = -1e30
norm_eps = 1e-05
adam_eps = 1e-08

f32 = jnp.float32
bf16 = jnp.bfloat16
sds = jax.ShapeDtypeStruct
VMEM = pltpu.VMEM


def cdot(left, right, left_dim, right_dim, precision=None):
    return lax.dot_general(
        left,
        right,
        (((left_dim,), (right_dim,)), ((), ())),
        precision=precision,
        preferred_element_type=f32,
    )


def low_lanes(shape):
    return lax.broadcasted_iota(jnp.int32, shape, 1) < HEAD_DIM


def head_pair_rows(pair, with_ones):
    low = low_lanes(pair.shape)
    zero = jnp.zeros_like(pair)
    first = jnp.where(low, pair, zero)
    second = jnp.where(low, zero, pair)
    if with_ones:
        one = jnp.ones_like(pair)
        first = jnp.concatenate([first, jnp.where(low, one, zero)], axis=1)
        second = jnp.concatenate([second, jnp.where(low, zero, one)], axis=1)
    return jnp.concatenate([first, second], axis=0)


def row_mean(values):
    return jnp.sum(values, axis=1, keepdims=True) * (1.0 / values.shape[1])


def layer_kernel(
    lens,
    x_hbm,
    cot_hbm,
    wq_hbm,
    wk_hbm,
    wv_hbm,
    wo_hbm,
    w1_hbm,
    w2_hbm,
    bq,
    bv,
    bo,
    b1,
    b2,
    gains,
    shifts,
    down,
    up,
    mixed_hbm,
    midg_hbm,
    dq_hbm,
    dk_hbm,
    dv_hbm,
    dg_hbm,
    keep_out,
    send_out,
    x,
    cot,
    wq,
    wk,
    wv,
    wo,
    w1,
    w2,
    acat,
    bcat_q,
    bcat_v,
    brep_q,
    brep_v,
    rowv,
    qs,
    ks,
    vs,
    dn,
    probs,
    ctx,
    inv_l,
    dctx,
    act,
    slope,
    mixed,
    midg,
    dq,
    dk,
    dv,
    dg,
    g_down,
    g_up_q,
    g_up_v,
    flat,
    in_sem,
    w_sem,
    out_sem,
    *,
    wide,
):
    d_model = x.shape[1]
    n_bucket = x.shape[0] // BUCKET
    n_pair = d_model // LANES
    ff = w1.shape[1]
    rank = up.shape[1]

    def bucket_copy(i, src, dst, sem):
        rows = pl.ds(i * BUCKET, BUCKET)
        return pltpu.make_async_copy(src.at[rows, :], dst.at[rows, :], sem)

    weights = [(wq_hbm, wq), (wk_hbm, wk), (wv_hbm, wv), (wo_hbm, wo), (w1_hbm, w1), (w2_hbm, w2)]
    weight_copies = [pltpu.make_async_copy(s, d, w_sem.at[i]) for i, (s, d) in enumerate(weights)]
    x_copies = [bucket_copy(i, x_hbm, x, in_sem.at[i]) for i in range(n_bucket)]
    cot_copies = [bucket_copy(i, cot_hbm, cot, in_sem.at[n_bucket + i]) for i in range(n_bucket)]
    x_copies[0].start()
    for c in weight_copies[:4]:
        c.start()
    cot_copies[0].start()
    for c in weight_copies[4:]:
        c.start()
    for c in x_copies[1:] + cot_copies[1:]:
        c.start()

    down_q = down[0].astype(bf16)
    down_v = down[1].astype(bf16)
    r_i = lax.broadcasted_iota(jnp.int32, (rank, LANES), 0)
    l_i = lax.broadcasted_iota(jnp.int32, (rank, LANES), 1)
    acat[...] = (
        cdot(down_q, (l_i == r_i).astype(bf16), 1, 0)
        + cdot(down_v, (l_i == r_i + rank).astype(bf16), 1, 0)
    ).astype(bf16)
    up_q = up[0].astype(bf16).astype(f32) * adapter_scale
    up_v = up[1].astype(bf16).astype(f32) * adapter_scale
    bcat_q[...] = jnp.concatenate(
        [up_q, jnp.zeros((LANES - rank, d_model), f32)], axis=0
    ).astype(bf16)
    bcat_v[...] = jnp.concatenate(
        [jnp.zeros((rank, d_model), f32), up_v, jnp.zeros((LANES - 2 * rank, d_model), f32)], axis=0
    ).astype(bf16)
    brep_q[...] = jnp.concatenate([up_q] * (LANES // rank), axis=0).astype(bf16)
    brep_v[...] = jnp.concatenate([up_v] * (LANES // rank), axis=0).astype(bf16)
    seq = 0
    row0 = 0
    n_valid = 0
    for length in (LEN_A, LEN_B, LEN_C):
        for s in range(BUCKET // length):
            n = lens[seq]
            n_valid = n_valid + n
            rowv[row0 : row0 + length, :] = (
                lax.broadcasted_iota(jnp.int32, (length, LANES), 0) < n
            ).astype(f32)
            seq += 1
            row0 += length
    g_down[...] = jnp.zeros_like(g_down)
    g_up_q[...] = jnp.zeros_like(g_up_q)
    g_up_v[...] = jnp.zeros_like(g_up_v)

    def attend(length, first_seq, b, p, s):
        rows = slice(s * length, (s + 1) * length)
        cols = pl.ds(pl.multiple_of(p * LANES, LANES), LANES)
        key_rows = head_pair_rows(ks[rows, cols], False)
        val_rows = head_pair_rows(vs[rows, cols], True)
        lane = lax.broadcasted_iota(jnp.int32, (1, length), 1)
        bias = jnp.where(lane < lens[first_seq + s], 0.0, neg_large).astype(f32)
        scores = cdot(qs[rows, cols], key_rows, 1, 1)
        parts = []
        for h in range(2):
            sh = scores[:, h * length : (h + 1) * length] + bias
            parts.append(jnp.exp(sh - jnp.max(sh, axis=1, keepdims=True)).astype(bf16))
        e = jnp.concatenate(parts, axis=1)
        probs[pl.ds(pl.multiple_of(p * BUCKET + s * length, LANES), length), : 2 * length] = e
        out = cdot(e, val_rows, 1, 0)
        inv = 1.0 / out[:, LANES:]
        inv_l[rows, cols] = inv
        ctx[rows, cols] = (out[:, :LANES] * inv).astype(bf16)

    def attend_back(length, b, p, s):
        rows = slice(s * length, (s + 1) * length)
        grows = pl.ds(pl.multiple_of(b * BUCKET + s * length, LANES), length)
        cols = pl.ds(pl.multiple_of(p * LANES, LANES), LANES)
        key_rows = head_pair_rows(ks[rows, cols], False)
        val_rows = head_pair_rows(vs[rows, cols], True)
        dcf = dctx[rows, cols].astype(f32) * inv_l[rows, cols]
        dc = dcf.astype(bf16)
        inner = (-dcf * ctx[rows, cols].astype(f32)).astype(bf16)
        g = cdot(jnp.concatenate([dc, inner], axis=1), val_rows, 1, 1)
        e = probs[pl.ds(pl.multiple_of(p * BUCKET + s * length, LANES), length), : 2 * length]
        ds = (e.astype(f32) * g).astype(bf16)
        dq[grows, cols] = (cdot(ds, key_rows, 1, 0) * (HEAD_DIM**-0.5)).astype(bf16)
        low = low_lanes((length, LANES))
        rk = cdot(ds, qs[rows, cols], 0, 0)
        dk[grows, cols] = jnp.where(low, rk[:length], rk[length:]).astype(bf16)
        rv = cdot(e, dc, 0, 0)
        dv[grows, cols] = jnp.where(low, rv[:length], rv[length:]).astype(bf16)

    def chain(b, c):
        size = 256
        lrows = pl.ds(pl.multiple_of(c * size, size), size)
        grows = pl.ds(pl.multiple_of(b * BUCKET + c * size, size), size)
        ms = cdot(ctx[lrows, :], wo[...], 1, 0) + bo[...] + x[grows, :].astype(f32)
        xc = ms - row_mean(ms)
        r1 = lax.rsqrt(row_mean(xc * xc) + norm_eps)
        n1 = xc * r1
        normed = n1 * gains[0:1, :] + shifts[0:1, :]
        nl = normed.astype(bf16)
        step = 512
        for n in range(0, ff, step):
            h = cdot(nl, w1[:, n : n + step], 1, 0) + b1[:, n : n + step]
            cdf = 0.5 + 0.5 * lax.erf(h * (0.5**0.5))
            pdf = jnp.exp(h * h * -0.5) * 0.3989422804014327
            act[:, n : n + step] = (h * cdf).astype(bf16)
            slope[:, n : n + step] = (cdf + h * pdf).astype(bf16)
        fs = cdot(act[...], w2[...], 1, 0) + b2[...] + normed
        fc = fs - row_mean(fs)
        r2 = lax.rsqrt(row_mean(fc * fc) + norm_eps)
        n2 = fc * r2
        mixed[grows, :] = (n2 * gains[1:2, :] + shifts[1:2, :]).astype(bf16)
        rv = rowv[grows, :]
        e2 = cot[grows, :].astype(f32) * jnp.concatenate([rv] * n_pair, axis=1) * gains[1:2, :]
        fg = r2 * (e2 - row_mean(e2) - n2 * row_mean(e2 * n2))
        ol = fg.astype(bf16)
        for n in range(0, ff, step):
            da = cdot(ol, w2[n : n + step, :], 1, 1)
            act[:, n : n + step] = (
                da.astype(bf16).astype(f32) * slope[:, n : n + step].astype(f32)
            ).astype(bf16)
        ng = fg + cdot(act[...], w1[...], 1, 1)
        e1 = ng * gains[0:1, :]
        mg = r1 * (e1 - row_mean(e1) - n1 * row_mean(e1 * n1))
        midg[grows, :] = mg
        dctx[lrows, :] = cdot(mg.astype(bf16), wo[...], 1, 1).astype(bf16)

    outs = [
        (mixed, mixed_hbm),
        (midg, midg_hbm),
        (dq, dq_hbm),
        (dk, dk_hbm),
        (dv, dv_hbm),
        (dg, dg_hbm),
    ]

    def bucket(b, carry):
        rows = pl.ds(pl.multiple_of(b * BUCKET, BUCKET), BUCKET)

        def wait_bucket(src, dst, base):
            pltpu.make_async_copy(src.at[rows, :], dst.at[rows, :], in_sem.at[base + b]).wait()

        wait_bucket(x_hbm, x, 0)

        @pl.when(b == 0)
        def _():
            for c in weight_copies[:3]:
                c.wait()

        xb = x[rows, :]
        dnb = cdot(xb, acat[...], 1, 0).astype(bf16)
        dn[...] = dnb
        qs[...] = (
            (cdot(xb, wq[...], 1, 0) + bq[...] + cdot(dnb, bcat_q[...], 1, 0)).astype(bf16)
            * jnp.asarray(HEAD_DIM**-0.5, bf16)
        )
        ks[...] = cdot(xb, wk[...], 1, 0).astype(bf16)
        vs[...] = (cdot(xb, wv[...], 1, 0) + bv[...] + cdot(dnb, bcat_v[...], 1, 0)).astype(bf16)

        first = 0
        for i, length in enumerate((LEN_A, LEN_B, LEN_C)):
            count = BUCKET // length

            @pl.when(b == i)
            def _(length=length, first=first, count=count):
                def pair(p, carry):
                    for s in range(count):
                        attend(length, first, b, p, s)
                    return carry

                lax.fori_loop(0, n_pair, pair, 0)

            first += count

        wait_bucket(cot_hbm, cot, n_bucket)

        @pl.when(b == 0)
        def _():
            for c in weight_copies[3:]:
                c.wait()

        def chunk(c, carry):
            chain(b, c)
            return carry

        lax.fori_loop(0, 2, chunk, 0)

        for i, length in enumerate((LEN_A, LEN_B, LEN_C)):
            count = BUCKET // length

            @pl.when(b == i)
            def _(length=length, count=count):
                def pair(p, carry):
                    for s in range(count):
                        attend_back(length, b, p, s)
                    return carry

                lax.fori_loop(0, n_pair, pair, 0)

        dqb = dq[rows, :]
        dvb = dv[rows, :]
        dgb = jnp.concatenate(
            [cdot(dqb, brep_q[...], 1, 1).astype(bf16), cdot(dvb, brep_v[...], 1, 1).astype(bf16)],
            axis=1,
        )
        dg[rows, :] = dgb
        g_down[...] += cdot(x[rows, :], dgb, 0, 0)
        dnb2 = dn[...]
        g_up_q[...] += cdot(dnb2, dqb, 0, 0)
        g_up_v[...] += cdot(dnb2, dvb, 0, 0)
        for i, (src, dst) in enumerate(outs):
            pltpu.make_async_copy(src.at[rows, :], dst.at[rows, :], out_sem.at[i * n_bucket + b]).start()
        return carry

    lax.fori_loop(0, n_bucket, bucket, 0)

    group = LANES // rank
    half_rows = d_model // group
    up_rows = d_model // LANES
    row_i = lax.broadcasted_iota(jnp.int32, (d_model, LANES), 0)
    lane_i = lax.broadcasted_iota(jnp.int32, (d_model, LANES), 1)
    pick = (row_i % group) == (lane_i // rank)
    for j in range(2):
        part = jnp.where(pick, g_down[:, j * LANES : (j + 1) * LANES], 0.0)
        flat[j * half_rows : (j + 1) * half_rows, :] = jnp.sum(
            part.reshape(half_rows, group, LANES), axis=1
        )
        src = (g_up_q, g_up_v)[j]
        base = 2 * half_rows + j * rank * up_rows
        for cb in range(up_rows):
            flat[pl.ds(base + cb, rank, stride=up_rows), :] = adapter_scale * (
                src[j * rank : (j + 1) * rank, cb * LANES : (cb + 1) * LANES]
            )
    core = lax.rem(lax.axis_index("wide"), 2)
    n_rows = flat.shape[0]
    chunk_rows = n_rows // wide
    unit = 8 if chunk_rows % 8 == 0 else 1
    for h in range(wide // 2):
        for k in range(0, chunk_rows, unit):
            at = h * chunk_rows + k
            mine = 2 * h * chunk_rows + k + core * chunk_rows
            other = 2 * h * chunk_rows + k + (1 - core) * chunk_rows
            if unit == 8:
                mine = pl.multiple_of(mine, 8)
                other = pl.multiple_of(other, 8)
            keep_out[at : at + unit, :] = flat[pl.ds(mine, unit), :]
            send_out[at : at + unit, :] = flat[pl.ds(other, unit), :]
    total = jnp.full((8, LANES), n_valid, jnp.int32).astype(f32)
    keep_out[n_rows // 2 :, :] = total
    send_out[n_rows // 2 :, :] = total
    for i, (src, dst) in enumerate(outs):
        for j in range(n_bucket):
            bucket_copy(j, src, dst, out_sem.at[i * n_bucket + j]).wait()


def layer(lens, x, cot, ws, vecs, gains, shifts, down, up, wide):
    t, d = x.shape
    ff = ws[4].shape[1]
    rank = up.shape[1]
    n_rows = 2 * down.size // LANES
    n_bucket = t // BUCKET
    any_spec = pl.BlockSpec(memory_space=pl.ANY)
    vm = pl.BlockSpec(memory_space=VMEM)
    ops = [lens, x, cot, *ws, *vecs, gains, shifts, down, up]
    in_specs = (
        [pl.BlockSpec(memory_space=pltpu.SMEM)] + [any_spec] * 8 + [vm] * (len(vecs) + 4)
    )
    out_shape = [
        sds((t, d), bf16),
        sds((t, d), f32),
        sds((t, d), bf16),
        sds((t, d), bf16),
        sds((t, d), bf16),
        sds((t, 2 * LANES), bf16),
        sds((n_rows // 2 + 8, LANES), f32),
        sds((n_rows // 2 + 8, LANES), f32),
    ]
    dma = pltpu.SemaphoreType.DMA
    scratch = [
        VMEM((t, d), bf16),
        VMEM((t, d), bf16),
        VMEM((d, d), bf16),
        VMEM((d, d), bf16),
        VMEM((d, d), bf16),
        VMEM((d, d), bf16),
        VMEM((d, ff), bf16),
        VMEM((ff, d), bf16),
        VMEM((d, LANES), bf16),
        VMEM((LANES, d), bf16),
        VMEM((LANES, d), bf16),
        VMEM((LANES, d), bf16),
        VMEM((LANES, d), bf16),
        VMEM((t, LANES), f32),
        VMEM((BUCKET, d), bf16),
        VMEM((BUCKET, d), bf16),
        VMEM((BUCKET, d), bf16),
        VMEM((BUCKET, LANES), bf16),
        VMEM((d // LANES * BUCKET, 2 * LEN_C), bf16),
        VMEM((BUCKET, d), bf16),
        VMEM((BUCKET, d), f32),
        VMEM((BUCKET, d), bf16),
        VMEM((256, ff), bf16),
        VMEM((256, ff), bf16),
        VMEM((t, d), bf16),
        VMEM((t, d), f32),
        VMEM((t, d), bf16),
        VMEM((t, d), bf16),
        VMEM((t, d), bf16),
        VMEM((t, 2 * LANES), bf16),
        VMEM((d, 2 * LANES), f32),
        VMEM((LANES, d), f32),
        VMEM((LANES, d), f32),
        VMEM((n_rows, LANES), f32),
        dma((2 * n_bucket,)),
        dma((6,)),
        dma((6 * n_bucket,)),
    ]
    body = lambda *refs: layer_kernel(*refs, wide=wide)
    return pl.pallas_call(
        body,
        out_shape=out_shape,
        in_specs=in_specs,
        out_specs=[any_spec] * 6 + [vm] * 2,
        scratch_shapes=scratch,
        compiler_params=pltpu.CompilerParams(vmem_limit_bytes=63 << 20),
        name="layer",
    )(*ops)


def token_kernel(mg, dq, dk, dv, dg, wq, wk, wv, down, out):
    down_q = down[0].astype(bf16)
    down_v = down[1].astype(bf16)
    acc = mg[...] + cdot(dq[...], wq[...], 1, 1)
    acc = acc + cdot(dk[...], wk[...], 1, 1)
    acc = acc + cdot(dv[...], wv[...], 1, 1)
    rank = down.shape[2]
    acc = acc + cdot(dg[:, :rank], down_q, 1, 1)
    acc = acc + cdot(dg[:, LANES : LANES + rank], down_v, 1, 1)
    out[...] = acc.astype(bf16)


def token_gradient(mg, dq, dk, dv, dg, wq, wk, wv, down):
    t, d = mg.shape
    size = 256
    row = lambda i: (i, 0)
    fixed = lambda i: (0, 0)
    return pl.pallas_call(
        token_kernel,
        grid=(t // size,),
        out_shape=sds((t, d), bf16),
        in_specs=[
            pl.BlockSpec((size, d), row),
            pl.BlockSpec((size, d), row),
            pl.BlockSpec((size, d), row),
            pl.BlockSpec((size, d), row),
            pl.BlockSpec((size, 2 * LANES), row),
            pl.BlockSpec((d, d), fixed),
            pl.BlockSpec((d, d), fixed),
            pl.BlockSpec((d, d), fixed),
            pl.BlockSpec(down.shape, lambda i: (0, 0, 0)),
        ],
        out_specs=pl.BlockSpec((size, d), row),
        compiler_params=pltpu.CompilerParams(vmem_limit_bytes=24 << 20),
        cost_estimate=pl.CostEstimate(
            flops=6 * t * d * d, bytes_accessed=14 * t * d, transcendentals=0
        ),
        name="token_gradient",
    )(mg, dq, dk, dv, dg, wq, wk, wv, down)


def digit_groups(size, first):
    bits = size.bit_length() - 1
    groups = []
    at = first
    while at < bits:
        n = min(2, bits - at)
        groups.append((at, n))
        at += n
    return groups


def swap_perm(size, mask):
    return [(i, i ^ mask) for i in range(size)]


def exchange(values, axis, size, group):
    low, n = group
    return [values] + [
        lax.ppermute(values, axis, swap_perm(size, j << low)) for j in range(1, 1 << n)
    ]


def tree_sum(parts):
    while len(parts) > 1:
        parts = [parts[i] + parts[i + 1] for i in range(0, len(parts), 2)]
    return parts[0]


def in_order(parts, digit):
    parts = list(parts)
    n = len(parts).bit_length() - 1
    for bit in range(n):
        flip = (digit >> bit) & 1
        parts = [jnp.where(flip == 1, parts[i ^ (1 << bit)], parts[i]) for i in range(len(parts))]
    return parts


def per_device(
    tokens,
    cotangent,
    valid_token_length,
    query_weight_matrix,
    key_weight_matrix,
    value_weight_matrix,
    attention_output_weight,
    inner_ffn_weight,
    outer_ffn_weight,
    query_bias_vector,
    value_bias_vector,
    attention_output_bias,
    hidden_ffn_bias,
    ffn_output_bias,
    layer_norm_gains,
    layer_norm_biases,
    adapter_down_factors,
    adapter_up_factors,
    first_moment_estimate,
    second_moment_estimate,
    first_decay_factor,
    second_decay_factor,
    optimizer_step_number,
):
    dp = lax.axis_size("dp")
    wide = lax.axis_size("wide")
    place = lax.axis_index("wide")
    core = place % 2
    n_rows = 2 * adapter_down_factors.size // LANES
    chunk_rows = n_rows // wide

    moments = jnp.concatenate(
        [first_moment_estimate.reshape(chunk_rows, LANES), second_moment_estimate.reshape(chunk_rows, LANES)],
        axis=0,
    )[None]
    for low, n in digit_groups(wide, 1):
        parts = exchange(moments, "wide", wide, (low, n))
        moments = jnp.concatenate(in_order(parts, place >> low), axis=0)
    first_half = moments[:, :chunk_rows].reshape(n_rows // 2, LANES)
    second_half = moments[:, chunk_rows:].reshape(n_rows // 2, LANES)

    params = jnp.concatenate(
        [adapter_down_factors.reshape(-1), adapter_up_factors.reshape(-1)]
    ).reshape(wide // 2, 2, chunk_rows, LANES)
    own_params = lax.dynamic_index_in_dim(params, core, 1, keepdims=False).reshape(n_rows // 2, LANES)

    mixed, midg, dq, dk, dv, dg, keep, send = layer(
        valid_token_length,
        tokens,
        cotangent,
        (
            query_weight_matrix,
            key_weight_matrix,
            value_weight_matrix,
            attention_output_weight,
            inner_ffn_weight,
            outer_ffn_weight,
        ),
        tuple(
            v.reshape(1, -1)
            for v in (
                query_bias_vector,
                value_bias_vector,
                attention_output_bias,
                hidden_ffn_bias,
                ffn_output_bias,
            )
        ),
        layer_norm_gains,
        layer_norm_biases,
        adapter_down_factors,
        adapter_up_factors,
        wide,
    )

    grad = keep + lax.ppermute(send, "wide", swap_perm(wide, 1))
    for group in digit_groups(dp, 0):
        grad = tree_sum(exchange(grad, "dp", dp, group))
    for group in digit_groups(wide, 1):
        grad = tree_sum(exchange(grad, "wide", wide, group))

    input_token_gradient = token_gradient(
        midg,
        dq,
        dk,
        dv,
        dg,
        query_weight_matrix,
        key_weight_matrix,
        value_weight_matrix,
        adapter_down_factors,
    )

    count = grad[n_rows // 2, 0]
    gradient = grad[: n_rows // 2] / count
    beta_one = first_decay_factor[0]
    beta_two = second_decay_factor[0]
    step = optimizer_step_number[0].astype(f32)
    inside_first = lax.broadcasted_iota(jnp.int32, (n_rows // 2, LANES), 0) < n_rows // 4
    step_rate = jnp.where(inside_first, rate_first, rate_second)
    decay_rate = jnp.where(inside_first, decay_first, decay_second)
    new_first = beta_one * first_half + (1.0 - beta_one) * gradient
    new_second = beta_two * second_half + (1.0 - beta_two) * gradient * gradient
    first_hat = new_first / (1.0 - jnp.power(beta_one, step))
    second_hat = new_second / (1.0 - jnp.power(beta_two, step))
    new_params = own_params * (1.0 - step_rate * decay_rate) - step_rate * first_hat / (
        jnp.sqrt(second_hat) + adam_eps
    )
    own = (place // 2) * chunk_rows
    updated_first = lax.dynamic_slice_in_dim(new_first, own, chunk_rows, 0).reshape(-1)
    updated_second = lax.dynamic_slice_in_dim(new_second, own, chunk_rows, 0).reshape(-1)
    other_params = lax.ppermute(new_params, "wide", swap_perm(wide, 1))
    halves = [
        v.reshape(wide // 2, 1, chunk_rows, LANES) for v in in_order([new_params, other_params], core)
    ]
    whole = jnp.concatenate(halves, axis=1).reshape(-1)
    updated_down = whole[: adapter_down_factors.size].reshape(adapter_down_factors.shape)
    updated_up = whole[adapter_down_factors.size :].reshape(adapter_up_factors.shape)
    return (mixed, input_token_gradient, updated_down, updated_up, updated_first, updated_second)


def solution(mesh):
    rows = P(("dp", "wide"), None)
    placed = (rows, rows, P(("dp", "wide"))) + (P(),) * 15 + (P("wide"), P("wide")) + (P(),) * 3
    return jax.shard_map(
        per_device,
        mesh=mesh,
        in_specs=placed,
        out_specs=(rows, rows, P(), P(), P("wide"), P("wide")),
        check_vma=False,
    )
```

```python
import jax
import jax.numpy as jnp
from jax import lax
from jax.experimental import pallas as pl
from jax.experimental.pallas import tpu as pltpu
from jax.sharding import PartitionSpec as P

HEADS = 12
HEAD_DIM = 64
LEN_A = 128
LEN_B = 256
LEN_C = 512
BUCKET = 512
LANES = 128

adapter_scale = 2.0
rate_first = 0.005
rate_second = 0.08
decay_first = 0.05
decay_second = 0.01
neg_large = -1e30
norm_eps = 1e-05
adam_eps = 1e-08

f32 = jnp.float32
bf16 = jnp.bfloat16
sds = jax.ShapeDtypeStruct
VMEM = pltpu.VMEM


def cdot(left, right, left_dim, right_dim, precision=None):
    return lax.dot_general(
        left,
        right,
        (((left_dim,), (right_dim,)), ((), ())),
        precision=precision,
        preferred_element_type=f32,
    )


def low_lanes(shape):
    return lax.broadcasted_iota(jnp.int32, shape, 1) < HEAD_DIM


def head_pair_rows(pair, with_ones):
    low = low_lanes(pair.shape)
    zero = jnp.zeros_like(pair)
    first = jnp.where(low, pair, zero)
    second = jnp.where(low, zero, pair)
    if with_ones:
        one = jnp.ones_like(pair)
        first = jnp.concatenate([first, jnp.where(low, one, zero)], axis=1)
        second = jnp.concatenate([second, jnp.where(low, zero, one)], axis=1)
    return jnp.concatenate([first, second], axis=0)


def row_mean(values):
    return jnp.sum(values, axis=1, keepdims=True) * (1.0 / values.shape[1])


def lane_is_rank(rank):
    shape = (rank, LANES)
    return lax.broadcasted_iota(jnp.int32, shape, 1) % rank == lax.broadcasted_iota(
        jnp.int32, shape, 0
    )


def lane_is_feature(rows, rank):
    shape = (rows, LANES)
    return lax.broadcasted_iota(jnp.int32, shape, 0) % (LANES // rank) == (
        lax.broadcasted_iota(jnp.int32, shape, 1) // rank
    )


def flatten_pair(flat, j, spread, up, scale):
    rank, width = up.shape
    group = LANES // rank
    down_rows = width // group
    part = jnp.where(lane_is_feature(width, rank), spread, 0.0)
    flat[j * down_rows : (j + 1) * down_rows, :] = jnp.sum(
        part.reshape(down_rows, group, LANES), axis=1
    )
    up_rows = width // LANES
    base = 2 * down_rows + j * rank * up_rows
    for cb in range(up_rows):
        flat[pl.ds(base + cb, rank, stride=up_rows), :] = (
            scale * up[:, cb * LANES : (cb + 1) * LANES]
        )


def row_moves(wide, chunk_rows):
    unit = 8 if chunk_rows % 8 == 0 else 1
    for h in range(wide // 2):
        for k in range(0, chunk_rows, unit):
            yield h * chunk_rows + k, 2 * h * chunk_rows + k, unit


def aligned(row, unit):
    return pl.multiple_of(row, unit) if unit > 1 else row


def split_half(flat, out, core, wide):
    chunk_rows = flat.shape[0] // wide
    for at, row, unit in row_moves(wide, chunk_rows):
        out[at : at + unit, :] = flat[pl.ds(aligned(row + core * chunk_rows, unit), unit), :]


def layer_kernel(
    lens,
    x_hbm,
    cot_hbm,
    wq_hbm,
    wk_hbm,
    wv_hbm,
    wo_hbm,
    w1_hbm,
    w2_hbm,
    bq,
    bv,
    bo,
    b1,
    b2,
    gains,
    shifts,
    down_t,
    up,
    mixed_hbm,
    midg_hbm,
    dq_hbm,
    dk_hbm,
    dv_hbm,
    dg_hbm,
    keep_out,
    send_out,
    params_out,
    x,
    cot,
    wq,
    wk,
    wv,
    wo,
    w1,
    w2,
    acat,
    bcat_q,
    bcat_v,
    brep_q,
    brep_v,
    rowv,
    qs,
    ks,
    vs,
    dn,
    probs,
    ctx,
    inv_l,
    dctx,
    act,
    slope,
    mixed,
    midg,
    dq,
    dk,
    dv,
    dg,
    g_down,
    g_up_q,
    g_up_v,
    flat,
    in_sem,
    w_sem,
    out_sem,
    *,
    wide,
):
    d_model = x.shape[1]
    n_bucket = x.shape[0] // BUCKET
    n_pair = d_model // LANES
    ff = w1.shape[1]
    rank = up.shape[1]
    core = lax.rem(lax.axis_index("wide"), 2)

    def bucket_copy(i, src, dst, sem):
        rows = pl.ds(i * BUCKET, BUCKET)
        return pltpu.make_async_copy(src.at[rows, :], dst.at[rows, :], sem)

    weights = [(wq_hbm, wq), (wk_hbm, wk), (wv_hbm, wv), (wo_hbm, wo), (w1_hbm, w1), (w2_hbm, w2)]
    weight_copies = [pltpu.make_async_copy(s, d, w_sem.at[i]) for i, (s, d) in enumerate(weights)]
    x_copies = [bucket_copy(i, x_hbm, x, in_sem.at[i]) for i in range(n_bucket)]
    cot_copies = [bucket_copy(i, cot_hbm, cot, in_sem.at[n_bucket + i]) for i in range(n_bucket)]
    x_copies[0].start()
    for c in weight_copies[:4]:
        c.start()
    cot_copies[0].start()
    for c in weight_copies[4:]:
        c.start()
    for c in x_copies[1:] + cot_copies[1:]:
        c.start()

    acat[...] = jnp.concatenate(
        [down_t[0], down_t[1], jnp.zeros((LANES - 2 * rank, d_model), f32)], axis=0
    ).astype(bf16)
    up_q = up[0].astype(bf16).astype(f32) * adapter_scale
    up_v = up[1].astype(bf16).astype(f32) * adapter_scale
    bcat_q[...] = jnp.concatenate(
        [up_q, jnp.zeros((LANES - rank, d_model), f32)], axis=0
    ).astype(bf16)
    bcat_v[...] = jnp.concatenate(
        [jnp.zeros((rank, d_model), f32), up_v, jnp.zeros((LANES - 2 * rank, d_model), f32)], axis=0
    ).astype(bf16)
    brep_q[...] = jnp.concatenate([up_q] * (LANES // rank), axis=0).astype(bf16)
    brep_v[...] = jnp.concatenate([up_v] * (LANES // rank), axis=0).astype(bf16)
    for j in range(2):
        spread = cdot(down_t[j], lane_is_rank(rank).astype(f32), 0, 0, lax.Precision.HIGHEST)
        flatten_pair(flat, j, spread, up[j], 1.0)
    split_half(flat, params_out, core, wide)
    seq = 0
    row0 = 0
    n_valid = 0
    for length in (LEN_A, LEN_B, LEN_C):
        for s in range(BUCKET // length):
            n = lens[seq]
            n_valid = n_valid + n
            rowv[row0 : row0 + length, :] = (
                lax.broadcasted_iota(jnp.int32, (length, LANES), 0) < n
            ).astype(f32)
            seq += 1
            row0 += length
    g_down[...] = jnp.zeros_like(g_down)
    g_up_q[...] = jnp.zeros_like(g_up_q)
    g_up_v[...] = jnp.zeros_like(g_up_v)

    def attend(length, first_seq, b, p, s):
        rows = slice(s * length, (s + 1) * length)
        cols = pl.ds(pl.multiple_of(p * LANES, LANES), LANES)
        key_rows = head_pair_rows(ks[rows, cols], False)
        val_rows = head_pair_rows(vs[rows, cols], True)
        lane = lax.broadcasted_iota(jnp.int32, (1, length), 1)
        bias = jnp.where(lane < lens[first_seq + s], 0.0, neg_large).astype(f32)
        scores = cdot(qs[rows, cols], key_rows, 1, 1)
        parts = []
        for h in range(2):
            sh = scores[:, h * length : (h + 1) * length] + bias
            parts.append(jnp.exp(sh - jnp.max(sh, axis=1, keepdims=True)).astype(bf16))
        e = jnp.concatenate(parts, axis=1)
        probs[pl.ds(pl.multiple_of(p * BUCKET + s * length, LANES), length), : 2 * length] = e
        out = cdot(e, val_rows, 1, 0)
        inv = 1.0 / out[:, LANES:]
        inv_l[rows, cols] = inv
        ctx[rows, cols] = (out[:, :LANES] * inv).astype(bf16)

    def attend_back(length, b, p, s):
        rows = slice(s * length, (s + 1) * length)
        grows = pl.ds(pl.multiple_of(b * BUCKET + s * length, LANES), length)
        cols = pl.ds(pl.multiple_of(p * LANES, LANES), LANES)
        key_rows = head_pair_rows(ks[rows, cols], False)
        val_rows = head_pair_rows(vs[rows, cols], True)
        dcf = dctx[rows, cols].astype(f32) * inv_l[rows, cols]
        dc = dcf.astype(bf16)
        inner = (-dcf * ctx[rows, cols].astype(f32)).astype(bf16)
        g = cdot(jnp.concatenate([dc, inner], axis=1), val_rows, 1, 1)
        e = probs[pl.ds(pl.multiple_of(p * BUCKET + s * length, LANES), length), : 2 * length]
        ds = (e.astype(f32) * g).astype(bf16)
        dq[grows, cols] = (cdot(ds, key_rows, 1, 0) * (HEAD_DIM**-0.5)).astype(bf16)
        low = low_lanes((length, LANES))
        rk = cdot(ds, qs[rows, cols], 0, 0)
        dk[grows, cols] = jnp.where(low, rk[:length], rk[length:]).astype(bf16)
        rv = cdot(e, dc, 0, 0)
        dv[grows, cols] = jnp.where(low, rv[:length], rv[length:]).astype(bf16)

    def chain(b, c):
        size = 256
        lrows = pl.ds(pl.multiple_of(c * size, size), size)
        grows = pl.ds(pl.multiple_of(b * BUCKET + c * size, size), size)
        ms = cdot(ctx[lrows, :], wo[...], 1, 0) + bo[...][None] + x[grows, :].astype(f32)
        xc = ms - row_mean(ms)
        r1 = lax.rsqrt(row_mean(xc * xc) + norm_eps)
        n1 = xc * r1
        normed = n1 * gains[0:1, :] + shifts[0:1, :]
        nl = normed.astype(bf16)
        step = 512
        for n in range(0, ff, step):
            h = cdot(nl, w1[:, n : n + step], 1, 0) + b1[n : n + step][None]
            cdf = 0.5 + 0.5 * lax.erf(h * (0.5**0.5))
            pdf = jnp.exp(h * h * -0.5) * 0.3989422804014327
            act[:, n : n + step] = (h * cdf).astype(bf16)
            slope[:, n : n + step] = (cdf + h * pdf).astype(bf16)
        fs = cdot(act[...], w2[...], 1, 0) + b2[...][None] + normed
        fc = fs - row_mean(fs)
        r2 = lax.rsqrt(row_mean(fc * fc) + norm_eps)
        n2 = fc * r2
        mixed[grows, :] = (n2 * gains[1:2, :] + shifts[1:2, :]).astype(bf16)
        rv = rowv[grows, :]
        e2 = cot[grows, :].astype(f32) * jnp.concatenate([rv] * n_pair, axis=1) * gains[1:2, :]
        fg = r2 * (e2 - row_mean(e2) - n2 * row_mean(e2 * n2))
        ol = fg.astype(bf16)
        for n in range(0, ff, step):
            da = cdot(ol, w2[n : n + step, :], 1, 1)
            act[:, n : n + step] = (
                da.astype(bf16).astype(f32) * slope[:, n : n + step].astype(f32)
            ).astype(bf16)
        ng = fg + cdot(act[...], w1[...], 1, 1)
        e1 = ng * gains[0:1, :]
        mg = r1 * (e1 - row_mean(e1) - n1 * row_mean(e1 * n1))
        midg[grows, :] = mg
        dctx[lrows, :] = cdot(mg.astype(bf16), wo[...], 1, 1).astype(bf16)

    outs = [
        (mixed, mixed_hbm),
        (midg, midg_hbm),
        (dq, dq_hbm),
        (dk, dk_hbm),
        (dv, dv_hbm),
        (dg, dg_hbm),
    ]

    def bucket(b, carry):
        rows = pl.ds(pl.multiple_of(b * BUCKET, BUCKET), BUCKET)

        def wait_bucket(src, dst, base):
            pltpu.make_async_copy(src.at[rows, :], dst.at[rows, :], in_sem.at[base + b]).wait()

        wait_bucket(x_hbm, x, 0)

        @pl.when(b == 0)
        def _():
            for c in weight_copies[:3]:
                c.wait()

        xb = x[rows, :]
        dnb = cdot(xb, acat[...], 1, 1).astype(bf16)
        dn[...] = dnb
        qs[...] = (
            (cdot(xb, wq[...], 1, 0) + bq[...][None] + cdot(dnb, bcat_q[...], 1, 0)).astype(bf16)
            * jnp.asarray(HEAD_DIM**-0.5, bf16)
        )
        ks[...] = cdot(xb, wk[...], 1, 0).astype(bf16)
        vs[...] = (cdot(xb, wv[...], 1, 0) + bv[...][None] + cdot(dnb, bcat_v[...], 1, 0)).astype(bf16)

        first = 0
        for i, length in enumerate((LEN_A, LEN_B, LEN_C)):
            count = BUCKET // length

            @pl.when(b == i)
            def _(length=length, first=first, count=count):
                def pair(p, carry):
                    for s in range(count):
                        attend(length, first, b, p, s)
                    return carry

                lax.fori_loop(0, n_pair, pair, 0)

            first += count

        wait_bucket(cot_hbm, cot, n_bucket)

        @pl.when(b == 0)
        def _():
            for c in weight_copies[3:]:
                c.wait()

        def chunk(c, carry):
            chain(b, c)
            return carry

        lax.fori_loop(0, 2, chunk, 0)

        for i, length in enumerate((LEN_A, LEN_B, LEN_C)):
            count = BUCKET // length

            @pl.when(b == i)
            def _(length=length, count=count):
                def pair(p, carry):
                    for s in range(count):
                        attend_back(length, b, p, s)
                    return carry

                lax.fori_loop(0, n_pair, pair, 0)

        dqb = dq[rows, :]
        dvb = dv[rows, :]
        dgb = jnp.concatenate(
            [cdot(dqb, brep_q[...], 1, 1).astype(bf16), cdot(dvb, brep_v[...], 1, 1).astype(bf16)],
            axis=1,
        )
        dg[rows, :] = dgb
        g_down[...] += cdot(x[rows, :], dgb, 0, 0)
        dnb2 = dn[...]
        g_up_q[...] += cdot(dnb2, dqb, 0, 0)
        g_up_v[...] += cdot(dnb2, dvb, 0, 0)
        for i, (src, dst) in enumerate(outs):
            pltpu.make_async_copy(src.at[rows, :], dst.at[rows, :], out_sem.at[i * n_bucket + b]).start()
        return carry

    lax.fori_loop(0, n_bucket, bucket, 0)

    for j, src in enumerate((g_up_q, g_up_v)):
        flatten_pair(
            flat,
            j,
            g_down[:, j * LANES : (j + 1) * LANES],
            src[j * rank : (j + 1) * rank, :],
            adapter_scale,
        )
    n_rows = flat.shape[0]
    split_half(flat, keep_out, core, wide)
    split_half(flat, send_out, 1 - core, wide)
    total = jnp.full((8, LANES), n_valid, jnp.int32).astype(f32)
    keep_out[n_rows // 2 :, :] = total
    send_out[n_rows // 2 :, :] = total
    for i, (src, dst) in enumerate(outs):
        for j in range(n_bucket):
            bucket_copy(j, src, dst, out_sem.at[i * n_bucket + j]).wait()


def layer(lens, x, cot, ws, vecs, gains, shifts, down_t, up, wide):
    t, d = x.shape
    ff = ws[4].shape[1]
    rank = up.shape[1]
    n_rows = 2 * down_t.size // LANES
    n_bucket = t // BUCKET
    any_spec = pl.BlockSpec(memory_space=pl.ANY)
    vm = pl.BlockSpec(memory_space=VMEM)
    ops = [lens, x, cot, *ws, *vecs, gains, shifts, down_t, up]
    in_specs = (
        [pl.BlockSpec(memory_space=pltpu.SMEM)] + [any_spec] * 8 + [vm] * (len(vecs) + 4)
    )
    out_shape = [
        sds((t, d), bf16),
        sds((t, d), f32),
        sds((t, d), bf16),
        sds((t, d), bf16),
        sds((t, d), bf16),
        sds((t, 2 * LANES), bf16),
        sds((n_rows // 2 + 8, LANES), f32),
        sds((n_rows // 2 + 8, LANES), f32),
        sds((n_rows // 2, LANES), f32),
    ]
    dma = pltpu.SemaphoreType.DMA
    scratch = [
        VMEM((t, d), bf16),
        VMEM((t, d), bf16),
        VMEM((d, d), bf16),
        VMEM((d, d), bf16),
        VMEM((d, d), bf16),
        VMEM((d, d), bf16),
        VMEM((d, ff), bf16),
        VMEM((ff, d), bf16),
        VMEM((LANES, d), bf16),
        VMEM((LANES, d), bf16),
        VMEM((LANES, d), bf16),
        VMEM((LANES, d), bf16),
        VMEM((LANES, d), bf16),
        VMEM((t, LANES), f32),
        VMEM((BUCKET, d), bf16),
        VMEM((BUCKET, d), bf16),
        VMEM((BUCKET, d), bf16),
        VMEM((BUCKET, LANES), bf16),
        VMEM((d // LANES * BUCKET, 2 * LEN_C), bf16),
        VMEM((BUCKET, d), bf16),
        VMEM((BUCKET, d), f32),
        VMEM((BUCKET, d), bf16),
        VMEM((256, ff), bf16),
        VMEM((256, ff), bf16),
        VMEM((t, d), bf16),
        VMEM((t, d), f32),
        VMEM((t, d), bf16),
        VMEM((t, d), bf16),
        VMEM((t, d), bf16),
        VMEM((t, 2 * LANES), bf16),
        VMEM((d, 2 * LANES), f32),
        VMEM((LANES, d), f32),
        VMEM((LANES, d), f32),
        VMEM((n_rows, LANES), f32),
        dma((2 * n_bucket,)),
        dma((6,)),
        dma((6 * n_bucket,)),
    ]
    body = lambda *refs: layer_kernel(*refs, wide=wide)
    return pl.pallas_call(
        body,
        out_shape=out_shape,
        in_specs=in_specs,
        out_specs=[any_spec] * 6 + [vm] * 3,
        scratch_shapes=scratch,
        compiler_params=pltpu.CompilerParams(vmem_limit_bytes=63 << 20),
        name="layer",
    )(*ops)


def token_kernel(prev, after, mg, dq, dk, dv, dg, wq, wk, wv, down_t, out):
    width = wq.shape[0]
    fill = jnp.zeros((LANES - down_t.shape[1], width), f32)
    down = jnp.concatenate([down_t[0], fill, down_t[1], fill], axis=0).astype(bf16)
    acc = mg[...] + cdot(dq[...], wq[...], 1, 1)
    acc = acc + cdot(dk[...], wk[...], 1, 1)
    acc = acc + cdot(dv[...], wv[...], 1, 1)
    acc = acc + cdot(dg[...], down, 1, 0)
    out[...] = acc.astype(bf16)


def token_gradient(prev, after, mg, dq, dk, dv, dg, wq, wk, wv, down_t, part, parts):
    t, d = mg.shape
    size = 256
    steps = t // size // parts
    row = lambda i: (i + part * steps, 0)
    fixed = lambda i: (0, 0)
    any_spec = pl.BlockSpec(memory_space=pl.ANY)
    args = (after, mg, dq, dk, dv, dg, wq, wk, wv, down_t)
    specs = [
        any_spec,
        pl.BlockSpec((size, d), row),
        pl.BlockSpec((size, d), row),
        pl.BlockSpec((size, d), row),
        pl.BlockSpec((size, d), row),
        pl.BlockSpec((size, 2 * LANES), row),
        pl.BlockSpec((d, d), fixed),
        pl.BlockSpec((d, d), fixed),
        pl.BlockSpec((d, d), fixed),
        pl.BlockSpec(down_t.shape, lambda i: (0, 0, 0)),
    ]
    if prev is None:
        body = lambda *refs: token_kernel(None, *refs)
        aliases = {}
    else:
        body = token_kernel
        args = (prev,) + args
        specs = [any_spec] + specs
        aliases = {0: 0}
    return pl.pallas_call(
        body,
        grid=(steps,),
        out_shape=sds((t, d), bf16),
        in_specs=specs,
        out_specs=pl.BlockSpec((size, d), row),
        input_output_aliases=aliases,
        compiler_params=pltpu.CompilerParams(vmem_limit_bytes=60 << 20),
        cost_estimate=pl.CostEstimate(
            flops=6 * t * d * d // parts, bytes_accessed=14 * t * d // parts, transcendentals=0
        ),
        name="token_gradient",
    )(*args)


def adam_kernel(beta_one, beta_two, step, *refs, n, held, wide, low):
    pieces = refs[:n]
    params, new_params, first_out, second_out, first, second, new_first, new_second = refs[n:]
    rows = params.shape[0]
    chunk_rows = 2 * rows // wide
    place = lax.axis_index("wide")
    digit = (place >> low) % n
    block = held * chunk_rows
    unit = 8 if block % 8 == 0 else 1
    for j, piece in enumerate(pieces):
        at = aligned((digit ^ j) * block, unit)
        first[pl.ds(at, block), :] = piece[rows + 8 : rows + 8 + block, :]
        second[pl.ds(at, block), :] = piece[rows + 8 + block : rows + 8 + 2 * block, :]
    total = tree_sum([p[: rows + 8, :] for p in pieces])
    gradient = total[:rows] / total[rows : rows + 1]
    b1 = jnp.full((8, LANES), beta_one[0], f32)
    b2 = jnp.full((8, LANES), beta_two[0], f32)
    count = step[0]
    power1 = jnp.ones((8, LANES), f32)
    power2 = power1
    square1, square2 = b1, b2
    for bit in range(16):
        on = ((count >> bit) & 1) == 1
        power1 = jnp.where(on, power1 * square1, power1)
        power2 = jnp.where(on, power2 * square2, power2)
        square1 = square1 * square1
        square2 = square2 * square2
    b1, b2 = b1[:1], b2[:1]
    m = b1 * first[...] + (1.0 - b1) * gradient
    v = b2 * second[...] + (1.0 - b2) * gradient * gradient
    inside_first = lax.broadcasted_iota(jnp.int32, (rows, LANES), 0) < rows // 2
    rate = jnp.where(inside_first, rate_first, rate_second)
    decay = jnp.where(inside_first, decay_first, decay_second)
    new_params[...] = params[...] * (1.0 - rate * decay) - rate * (m / (1.0 - power1[:1])) / (
        jnp.sqrt(v / (1.0 - power2[:1])) + adam_eps
    )
    new_first[...] = m
    new_second[...] = v
    own = (place // 2) * chunk_rows
    unit = 8 if chunk_rows % 8 == 0 else 1
    for k in range(0, chunk_rows, unit):
        at = aligned(own + k, unit)
        first_out[k : k + unit, :] = new_first[pl.ds(at, unit), :]
        second_out[k : k + unit, :] = new_second[pl.ds(at, unit), :]


def adam(beta_one, beta_two, step, pieces, params, held, wide, low):
    rows = params.shape[0]
    chunk_rows = 2 * rows // wide
    smem = pl.BlockSpec(memory_space=pltpu.SMEM)
    vm = pl.BlockSpec(memory_space=VMEM)
    n = len(pieces)
    return pl.pallas_call(
        lambda *refs: adam_kernel(*refs, n=n, held=held, wide=wide, low=low),
        out_shape=[sds((rows, LANES), f32)] + [sds((chunk_rows, LANES), f32)] * 2,
        in_specs=[smem] * 3 + [vm] * (n + 1),
        out_specs=[vm] * 3,
        scratch_shapes=[VMEM((rows, LANES), f32)] * 4,
        name="adam",
    )(beta_one, beta_two, step, *pieces, params)


def unflatten_kernel(own, other, down_t, up, flat, *, wide):
    core = lax.rem(lax.axis_index("wide"), 2)
    rank, width = up.shape[1:]
    chunk_rows = flat.shape[0] // wide
    for at, row, unit in row_moves(wide, chunk_rows):
        flat[pl.ds(aligned(row + core * chunk_rows, unit), unit), :] = own[at : at + unit, :]
        flat[pl.ds(aligned(row + (1 - core) * chunk_rows, unit), unit), :] = other[
            at : at + unit, :
        ]
    group = LANES // rank
    down_rows = width // group
    up_rows = width // LANES
    for j in range(2):
        spread = jnp.broadcast_to(
            flat[j * down_rows : (j + 1) * down_rows, :][:, None, :], (down_rows, group, LANES)
        ).reshape(width, LANES)
        part = jnp.where(lane_is_feature(width, rank), spread, 0.0)
        down_t[j] = cdot(lane_is_rank(rank).astype(f32), part, 1, 1, lax.Precision.HIGHEST)
        base = 2 * down_rows + j * rank * up_rows
        for cb in range(up_rows):
            up[j, :, cb * LANES : (cb + 1) * LANES] = flat[pl.ds(base + cb, rank, stride=up_rows), :]


def unflatten(own, other, down_shape, up_shape, wide):
    vm = pl.BlockSpec(memory_space=VMEM)
    return pl.pallas_call(
        lambda *refs: unflatten_kernel(*refs, wide=wide),
        out_shape=[sds(down_shape, f32), sds(up_shape, f32)],
        in_specs=[vm] * 2,
        out_specs=[vm] * 2,
        scratch_shapes=[VMEM((2 * own.shape[0], LANES), f32)],
        name="unflatten",
    )(own, other)


def digit_groups(size, first):
    bits = size.bit_length() - 1
    groups = []
    at = first
    while at < bits:
        n = min(2, bits - at)
        groups.append((at, n))
        at += n
    return groups


def swap_perm(size, mask):
    return [(i, i ^ mask) for i in range(size)]


def exchange(values, axis, size, group):
    low, n = group
    return [values] + [
        lax.ppermute(values, axis, swap_perm(size, j << low)) for j in range(1, 1 << n)
    ]


def tree_sum(parts):
    while len(parts) > 1:
        parts = [parts[i] + parts[i + 1] for i in range(0, len(parts), 2)]
    return parts[0]


def in_order(parts, digit):
    parts = list(parts)
    n = len(parts).bit_length() - 1
    for bit in range(n):
        flip = (digit >> bit) & 1
        parts = [jnp.where(flip == 1, parts[i ^ (1 << bit)], parts[i]) for i in range(len(parts))]
    return parts


def per_device(
    tokens,
    cotangent,
    valid_token_length,
    query_weight_matrix,
    key_weight_matrix,
    value_weight_matrix,
    attention_output_weight,
    inner_ffn_weight,
    outer_ffn_weight,
    query_bias_vector,
    value_bias_vector,
    attention_output_bias,
    hidden_ffn_bias,
    ffn_output_bias,
    layer_norm_gains,
    layer_norm_biases,
    adapter_down_factors,
    adapter_up_factors,
    first_moment_estimate,
    second_moment_estimate,
    first_decay_factor,
    second_decay_factor,
    optimizer_step_number,
):
    dp = lax.axis_size("dp")
    wide = lax.axis_size("wide")
    place = lax.axis_index("wide")
    n_rows = 2 * adapter_down_factors.size // LANES
    chunk_rows = n_rows // wide

    down_t = jnp.swapaxes(adapter_down_factors, 1, 2)
    mixed, midg, dq, dk, dv, dg, keep, send, own_params = layer(
        valid_token_length,
        tokens,
        cotangent,
        (
            query_weight_matrix,
            key_weight_matrix,
            value_weight_matrix,
            attention_output_weight,
            inner_ffn_weight,
            outer_ffn_weight,
        ),
        (
            query_bias_vector,
            value_bias_vector,
            attention_output_bias,
            hidden_ffn_bias,
            ffn_output_bias,
        ),
        layer_norm_gains,
        layer_norm_biases,
        down_t,
        adapter_up_factors,
        wide,
    )

    def token_part(prev, after, part):
        return token_gradient(
            prev,
            after,
            midg,
            dq,
            dk,
            dv,
            dg,
            query_weight_matrix,
            key_weight_matrix,
            value_weight_matrix,
            down_t,
            part,
            2,
        )

    grad = keep + lax.ppermute(send, "wide", swap_perm(wide, 1))
    token_grad = token_part(None, grad, 0)
    for group in digit_groups(dp, 0):
        grad = tree_sum(exchange(grad, "dp", dp, group))
    token_grad = token_part(token_grad, grad, 1)

    first = first_moment_estimate.reshape(chunk_rows, LANES)
    second = second_moment_estimate.reshape(chunk_rows, LANES)
    held = 1
    rows = n_rows // 2 + 8
    groups = digit_groups(wide, 1)
    for i, (low, n) in enumerate(groups):
        pieces = exchange(jnp.concatenate([grad, first, second], axis=0), "wide", wide, (low, n))
        if i + 1 < len(groups):
            grad = tree_sum([p[:rows] for p in pieces])
            block = held * chunk_rows
            pieces = in_order(pieces, place >> low)
            first = jnp.concatenate([p[rows : rows + block] for p in pieces], axis=0)
            second = jnp.concatenate([p[rows + block :] for p in pieces], axis=0)
            held *= len(pieces)
    new_params, updated_first, updated_second = adam(
        first_decay_factor,
        second_decay_factor,
        optimizer_step_number,
        pieces,
        own_params,
        held,
        wide,
        groups[-1][0],
    )
    other_params = lax.ppermute(new_params, "wide", swap_perm(wide, 1))
    updated_down_t, updated_up = unflatten(
        new_params, other_params, down_t.shape, adapter_up_factors.shape, wide
    )
    return (
        mixed,
        token_grad,
        jnp.swapaxes(updated_down_t, 1, 2),
        updated_up,
        updated_first.reshape(-1),
        updated_second.reshape(-1),
    )


def solution(mesh):
    rows = P(("dp", "wide"), None)
    placed = (rows, rows, P(("dp", "wide"))) + (P(),) * 15 + (P("wide"), P("wide")) + (P(),) * 3
    return jax.shard_map(
        per_device,
        mesh=mesh,
        in_specs=placed,
        out_specs=(rows, rows, P(), P(), P("wide"), P("wide")),
        check_vma=False,
    )
```

```python
import jax
import jax.numpy as jnp
from jax import lax
from jax.experimental import pallas as pl
from jax.experimental.pallas import tpu as pltpu
from jax.sharding import PartitionSpec as P

HEADS = 12
HEAD_DIM = 64
LEN_A = 128
LEN_B = 256
LEN_C = 512
BUCKET = 512
LANES = 128

adapter_scale = 2.0
rate_first = 0.005
rate_second = 0.08
decay_first = 0.05
decay_second = 0.01
neg_large = -1e30
norm_eps = 1e-05
adam_eps = 1e-08

f32 = jnp.float32
bf16 = jnp.bfloat16
sds = jax.ShapeDtypeStruct
VMEM = pltpu.VMEM


def cdot(left, right, left_dim, right_dim, precision=None):
    return lax.dot_general(
        left,
        right,
        (((left_dim,), (right_dim,)), ((), ())),
        precision=precision,
        preferred_element_type=f32,
    )


def low_lanes(shape):
    return lax.broadcasted_iota(jnp.int32, shape, 1) < HEAD_DIM


def head_pair_rows(pair, with_ones):
    low = low_lanes(pair.shape)
    zero = jnp.zeros_like(pair)
    first = jnp.where(low, pair, zero)
    second = jnp.where(low, zero, pair)
    if with_ones:
        one = jnp.ones_like(pair)
        first = jnp.concatenate([first, jnp.where(low, one, zero)], axis=1)
        second = jnp.concatenate([second, jnp.where(low, zero, one)], axis=1)
    return jnp.concatenate([first, second], axis=0)


def row_mean(values):
    return jnp.sum(values, axis=1, keepdims=True) * (1.0 / values.shape[1])


def lane_is_rank(rank):
    shape = (rank, LANES)
    return lax.broadcasted_iota(jnp.int32, shape, 1) % rank == lax.broadcasted_iota(
        jnp.int32, shape, 0
    )


def lane_is_feature(rows, rank):
    shape = (rows, LANES)
    return lax.broadcasted_iota(jnp.int32, shape, 0) % (LANES // rank) == (
        lax.broadcasted_iota(jnp.int32, shape, 1) // rank
    )


def flatten_pair(flat, j, spread, up, scale):
    rank, width = up.shape
    group = LANES // rank
    down_rows = width // group
    part = jnp.where(lane_is_feature(width, rank), spread, 0.0)
    flat[j * down_rows : (j + 1) * down_rows, :] = jnp.sum(
        part.reshape(down_rows, group, LANES), axis=1
    )
    up_rows = width // LANES
    base = 2 * down_rows + j * rank * up_rows
    for cb in range(up_rows):
        flat[pl.ds(base + cb, rank, stride=up_rows), :] = (
            scale * up[:, cb * LANES : (cb + 1) * LANES]
        )


def row_moves(wide, chunk_rows):
    unit = 8 if chunk_rows % 8 == 0 else 1
    for h in range(wide // 2):
        for k in range(0, chunk_rows, unit):
            yield h * chunk_rows + k, 2 * h * chunk_rows + k, unit


def aligned(row, unit):
    return pl.multiple_of(row, unit) if unit > 1 else row


def split_half(flat, out, core, wide):
    chunk_rows = flat.shape[0] // wide
    for at, row, unit in row_moves(wide, chunk_rows):
        out[at : at + unit, :] = flat[pl.ds(aligned(row + core * chunk_rows, unit), unit), :]


def layer_kernel(
    lens,
    x_hbm,
    cot_hbm,
    wq_hbm,
    wk_hbm,
    wv_hbm,
    wo_hbm,
    w1_hbm,
    w2_hbm,
    bq,
    bv,
    bo,
    b1,
    b2,
    gains,
    shifts,
    down_t,
    up,
    mixed_hbm,
    tokg_hbm,
    keep_out,
    send_out,
    x,
    cot,
    wq,
    wk,
    wv,
    wo,
    w1,
    w2,
    acat,
    brep_q,
    brep_v,
    rowv,
    qs,
    ks,
    vs,
    dn,
    probs,
    ctx,
    inv_l,
    dctx,
    act,
    slope,
    mixed,
    tokg,
    midg,
    dq,
    dk,
    dv,
    g_down,
    g_up_q,
    g_up_v,
    flat,
    in_sem,
    w_sem,
    out_sem,
    *,
    wide,
):
    d_model = x.shape[1]
    n_bucket = x.shape[0] // BUCKET
    n_pair = d_model // LANES
    ff = w1.shape[1]
    rank = up.shape[1]
    core = lax.rem(lax.axis_index("wide"), 2)

    def bucket_copy(i, src, dst, sem):
        rows = pl.ds(i * BUCKET, BUCKET)
        return pltpu.make_async_copy(src.at[rows, :], dst.at[rows, :], sem)

    weights = [(wq_hbm, wq), (wk_hbm, wk), (wv_hbm, wv), (wo_hbm, wo), (w1_hbm, w1), (w2_hbm, w2)]
    weight_copies = [pltpu.make_async_copy(s, d, w_sem.at[i]) for i, (s, d) in enumerate(weights)]
    x_copies = [bucket_copy(i, x_hbm, x, in_sem.at[i]) for i in range(n_bucket)]
    cot_copies = [bucket_copy(i, cot_hbm, cot, in_sem.at[n_bucket + i]) for i in range(n_bucket)]
    x_copies[0].start()
    for c in weight_copies[:4]:
        c.start()
    cot_copies[0].start()
    for c in weight_copies[4:]:
        c.start()
    for c in x_copies[1:] + cot_copies[1:]:
        c.start()

    acat[...] = jnp.concatenate(
        [down_t[0], down_t[1], jnp.zeros((LANES - 2 * rank, d_model), f32)], axis=0
    ).astype(bf16)
    up_q = up[0].astype(bf16).astype(f32) * adapter_scale
    up_v = up[1].astype(bf16).astype(f32) * adapter_scale
    brep_q[...] = jnp.concatenate([up_q] * (LANES // rank), axis=0).astype(bf16)
    brep_v[...] = jnp.concatenate([up_v] * (LANES // rank), axis=0).astype(bf16)
    seq = 0
    row0 = 0
    n_valid = 0
    for length in (LEN_A, LEN_B, LEN_C):
        for s in range(BUCKET // length):
            n = lens[seq]
            n_valid = n_valid + n
            rowv[row0 : row0 + length, :] = (
                lax.broadcasted_iota(jnp.int32, (length, LANES), 0) < n
            ).astype(f32)
            seq += 1
            row0 += length
    g_down[...] = jnp.zeros_like(g_down)
    g_up_q[...] = jnp.zeros_like(g_up_q)
    g_up_v[...] = jnp.zeros_like(g_up_v)

    def pair_at(p, row):
        if isinstance(p, int):
            return slice(p * LANES, (p + 1) * LANES), p * BUCKET + row
        return (
            pl.ds(pl.multiple_of(p * LANES, LANES), LANES),
            pl.multiple_of(p * BUCKET + row, LANES),
        )

    def each_pair(per_step, body):
        if per_step == n_pair:
            for p in range(n_pair):
                body(p, p)
            return

        def step_of(i, carry):
            for j in range(per_step):
                body(i * per_step + j, j)
            return carry

        lax.fori_loop(0, n_pair // per_step, step_of, 0)

    def attend(length, first_seq, p, s):
        rows = slice(s * length, (s + 1) * length)
        cols, prow = pair_at(p, s * length)
        key_rows = head_pair_rows(ks[rows, cols], False)
        val_rows = head_pair_rows(vs[rows, cols], True)
        lane = lax.broadcasted_iota(jnp.int32, (1, length), 1)
        bias = jnp.where(lane < lens[first_seq + s], 0.0, neg_large).astype(f32)
        scores = cdot(qs[rows, cols], key_rows, 1, 1)
        parts = []
        for h in range(2):
            sh = scores[:, h * length : (h + 1) * length] + bias
            parts.append(jnp.exp(sh - jnp.max(sh, axis=1, keepdims=True)).astype(bf16))
        e = jnp.concatenate(parts, axis=1)
        probs[pl.ds(prow, length), : 2 * length] = e
        out = cdot(e, val_rows, 1, 0)
        inv = 1.0 / out[:, LANES:]
        inv_l[rows, cols] = inv
        ctx[rows, cols] = (out[:, :LANES] * inv).astype(bf16)

    def attend_back(length, p, s, values_first):
        rows = slice(s * length, (s + 1) * length)
        cols, prow = pair_at(p, s * length)
        key_rows = head_pair_rows(ks[rows, cols], False)
        val_rows = head_pair_rows(vs[rows, cols], True)
        low = low_lanes((length, LANES))
        dcf = dctx[rows, cols].astype(f32) * inv_l[rows, cols]
        dc = dcf.astype(bf16)
        inner = (-dcf * ctx[rows, cols].astype(f32)).astype(bf16)
        e = probs[pl.ds(prow, length), : 2 * length]

        def value_part():
            rv = cdot(e, dc, 0, 0)
            dv[rows, cols] = jnp.where(low, rv[:length], rv[length:]).astype(bf16)

        if values_first:
            value_part()
        g = cdot(jnp.concatenate([dc, inner], axis=1), val_rows, 1, 1)
        ds = (e.astype(f32) * g).astype(bf16)
        dq[rows, cols] = (cdot(ds, key_rows, 1, 0) * (HEAD_DIM**-0.5)).astype(bf16)
        rk = cdot(ds, qs[rows, cols], 0, 0)
        dk[rows, cols] = jnp.where(low, rk[:length], rk[length:]).astype(bf16)
        if not values_first:
            value_part()

    size = 256
    n_chunk = 2
    ahead = (6, 6, 6)
    back = (3, 6, 3)
    step = 256

    def chain(b, first_row):
        chunks = range(n_chunk)
        lrows = [pl.ds(pl.multiple_of(first_row + c * size, size), size) for c in chunks]
        grows = [
            pl.ds(pl.multiple_of(b * BUCKET + first_row + c * size, size), size) for c in chunks
        ]

        def first_norm(c):
            ms = cdot(ctx[lrows[c], :], wo[...], 1, 0) + bo[...][None] + x[grows[c], :].astype(f32)
            xc = ms - row_mean(ms)
            r1 = lax.rsqrt(row_mean(xc * xc) + norm_eps)
            n1 = xc * r1
            return r1, n1, n1 * gains[0:1, :] + shifts[0:1, :]

        def inner_ffn(c, nl):
            for n in range(0, ff, step):
                h = cdot(nl, w1[:, n : n + step], 1, 0) + b1[n : n + step][None]
                cdf = 0.5 + 0.5 * lax.erf(h * (0.5**0.5))
                pdf = jnp.exp(h * h * -0.5) * 0.3989422804014327
                act[lrows[c], n : n + step] = (h * cdf).astype(bf16)
                slope[lrows[c], n : n + step] = (cdf + h * pdf).astype(bf16)

        def second_norm(c, normed):
            fs = cdot(act[lrows[c], :], w2[...], 1, 0) + b2[...][None] + normed
            fc = fs - row_mean(fs)
            r2 = lax.rsqrt(row_mean(fc * fc) + norm_eps)
            n2 = fc * r2
            mixed[lrows[c], :] = (n2 * gains[1:2, :] + shifts[1:2, :]).astype(bf16)
            rv = rowv[grows[c], :]
            e2 = cot[grows[c], :].astype(f32) * jnp.concatenate([rv] * n_pair, axis=1)
            e2 = e2 * gains[1:2, :]
            return r2 * (e2 - row_mean(e2) - n2 * row_mean(e2 * n2))

        def inner_back(c, ol):
            for n in range(0, ff, step):
                da = cdot(ol, w2[n : n + step, :], 1, 1).astype(bf16)
                act[lrows[c], n : n + step] = da * slope[lrows[c], n : n + step]

        def first_back(c, fg, r1, n1):
            e1 = (fg + cdot(act[lrows[c], :], w1[...], 1, 1)) * gains[0:1, :]
            mg = r1 * (e1 - row_mean(e1) - n1 * row_mean(e1 * n1))
            midg[lrows[c], :] = mg
            dctx[lrows[c], :] = cdot(mg.astype(bf16), wo[...], 1, 1).astype(bf16)

        firsts = [first_norm(c) for c in chunks]
        for c in chunks:
            inner_ffn(c, firsts[c][2].astype(bf16))
        grads = [second_norm(c, firsts[c][2]) for c in chunks]
        for c in chunks:
            inner_back(c, grads[c].astype(bf16))
        for c in chunks:
            first_back(c, grads[c], firsts[c][0], firsts[c][1])

    outs = [(mixed, mixed_hbm), (tokg, tokg_hbm)]

    def out_copy(i, b):
        rows = pl.ds(pl.multiple_of(b * BUCKET, BUCKET), BUCKET)
        src, dst = outs[i]
        return pltpu.make_async_copy(src, dst.at[rows, :], out_sem.at[i])

    def out_free(which, b):
        @pl.when(b > 0)
        def _():
            for i in which:
                out_copy(i, b - 1).wait()

    def bucket(b, carry):
        rows = pl.ds(pl.multiple_of(b * BUCKET, BUCKET), BUCKET)

        def wait_bucket(src, dst, base):
            pltpu.make_async_copy(src.at[rows, :], dst.at[rows, :], in_sem.at[base + b]).wait()

        wait_bucket(x_hbm, x, 0)

        @pl.when(b == 0)
        def _():
            for i, (w, low, high) in enumerate(((wq, down_t[0], up_q), (wk, None, None), (wv, down_t[1], up_v))):
                weight_copies[i].wait()
                if low is not None:
                    w[...] = (
                        w[...].astype(f32) + cdot(low.astype(bf16), high.astype(bf16), 0, 0)
                    ).astype(bf16)

        xb = x[rows, :]
        dnb = cdot(xb, acat[...], 1, 1).astype(bf16)
        dn[...] = dnb
        qs[...] = (cdot(xb, wq[...], 1, 0) + bq[...][None]).astype(bf16) * jnp.asarray(
            HEAD_DIM**-0.5, bf16
        )
        ks[...] = cdot(xb, wk[...], 1, 0).astype(bf16)
        vs[...] = (cdot(xb, wv[...], 1, 0) + bv[...][None]).astype(bf16)

        first = 0
        for i, length in enumerate((LEN_A, LEN_B, LEN_C)):
            count = BUCKET // length

            @pl.when(b == i)
            def _(i=i, length=length, first=first, count=count):
                def both(p, place):
                    for s in range(count):
                        attend(length, first, p, s)

                each_pair(ahead[i], both)

            first += count

        wait_bucket(cot_hbm, cot, n_bucket)

        @pl.when(b == 0)
        def _():
            for c in weight_copies[3:]:
                c.wait()

        out_free((0,), b)

        def chunk(c, carry):
            chain(b, c * (size * n_chunk))
            return carry

        lax.fori_loop(0, BUCKET // (size * n_chunk), chunk, 0)
        out_copy(0, b).start()

        for i, length in enumerate((LEN_A, LEN_B, LEN_C)):
            count = BUCKET // length

            @pl.when(b == i)
            def _(i=i, length=length, count=count):
                def both(p, place):
                    for s in range(count):
                        attend_back(length, p, s, (place * count + s) % 2 == 1)

                each_pair(back[i], both)

        out_free((1,), b)
        dqb = dq[...]
        dvb = dv[...]
        dgb = jnp.concatenate(
            [cdot(dqb, brep_q[...], 1, 1).astype(bf16), cdot(dvb, brep_v[...], 1, 1).astype(bf16)],
            axis=1,
        )
        g_down[...] += cdot(x[rows, :], dgb, 0, 0)
        dnb2 = dn[...]
        g_up_q[...] += cdot(dnb2, dqb, 0, 0)
        g_up_v[...] += cdot(dnb2, dvb, 0, 0)
        tokg[...] = (
            cdot(dqb, wq[...], 1, 1)
            + cdot(dk[...], wk[...], 1, 1)
            + cdot(dvb, wv[...], 1, 1)
            + midg[...]
        ).astype(bf16)
        out_copy(1, b).start()
        return carry

    lax.fori_loop(0, n_bucket, bucket, 0)

    for j, src in enumerate((g_up_q, g_up_v)):
        flatten_pair(
            flat,
            j,
            g_down[:, j * LANES : (j + 1) * LANES],
            src[j * rank : (j + 1) * rank, :],
            adapter_scale,
        )
    n_rows = flat.shape[0]
    split_half(flat, keep_out, core, wide)
    split_half(flat, send_out, 1 - core, wide)
    total = jnp.full((8, LANES), n_valid, jnp.int32).astype(f32)
    keep_out[n_rows // 2 :, :] = total
    send_out[n_rows // 2 :, :] = total
    for i in range(len(outs)):
        out_copy(i, n_bucket - 1).wait()


def layer(lens, x, cot, ws, vecs, gains, shifts, down_t, up, wide):
    t, d = x.shape
    ff = ws[4].shape[1]
    rank = up.shape[1]
    n_rows = 2 * down_t.size // LANES
    n_bucket = t // BUCKET
    any_spec = pl.BlockSpec(memory_space=pl.ANY)
    vm = pl.BlockSpec(memory_space=VMEM)
    ops = [lens, x, cot, *ws, *vecs, gains, shifts, down_t, up]
    in_specs = (
        [pl.BlockSpec(memory_space=pltpu.SMEM)] + [any_spec] * 8 + [vm] * (len(vecs) + 4)
    )
    out_shape = [
        sds((t, d), bf16),
        sds((t, d), bf16),
        sds((n_rows // 2 + 8, LANES), f32),
        sds((n_rows // 2 + 8, LANES), f32),
    ]
    dma = pltpu.SemaphoreType.DMA
    scratch = [
        VMEM((t, d), bf16),
        VMEM((t, d), bf16),
        VMEM((d, d), bf16),
        VMEM((d, d), bf16),
        VMEM((d, d), bf16),
        VMEM((d, d), bf16),
        VMEM((d, ff), bf16),
        VMEM((ff, d), bf16),
        VMEM((LANES, d), bf16),
        VMEM((LANES, d), bf16),
        VMEM((LANES, d), bf16),
        VMEM((t, LANES), f32),
        VMEM((BUCKET, d), bf16),
        VMEM((BUCKET, d), bf16),
        VMEM((BUCKET, d), bf16),
        VMEM((BUCKET, LANES), bf16),
        VMEM((d // LANES * BUCKET, 2 * LEN_C), bf16),
        VMEM((BUCKET, d), bf16),
        VMEM((BUCKET, d), f32),
        VMEM((BUCKET, d), bf16),
        VMEM((BUCKET, ff), bf16),
        VMEM((BUCKET, ff), bf16),
        VMEM((BUCKET, d), bf16),
        VMEM((BUCKET, d), bf16),
        VMEM((BUCKET, d), f32),
        VMEM((BUCKET, d), bf16),
        VMEM((BUCKET, d), bf16),
        VMEM((BUCKET, d), bf16),
        VMEM((d, 2 * LANES), f32),
        VMEM((LANES, d), f32),
        VMEM((LANES, d), f32),
        VMEM((n_rows, LANES), f32),
        dma((2 * n_bucket,)),
        dma((6,)),
        dma((2,)),
    ]
    body = lambda *refs: layer_kernel(*refs, wide=wide)
    return pl.pallas_call(
        body,
        out_shape=out_shape,
        in_specs=in_specs,
        out_specs=[any_spec] * 2 + [vm] * 2,
        scratch_shapes=scratch,
        compiler_params=pltpu.CompilerParams(vmem_limit_bytes=63 << 20),
        name="layer",
    )(*ops)


def update_kernel(
    beta_one, beta_two, step, own, other, down_t, up, new_down_t, new_up, first_out, second_out, *scratch, n, held, wide, low
):
    grads, first, second, moves = scratch
    rank, width = up.shape[1:]
    n_rows = grads.shape[0]
    rows = n_rows // 2
    chunk_rows = n_rows // wide
    place = lax.axis_index("wide")
    core = lax.rem(place, 2)
    digit = (place >> low) % n
    unit = 8 if chunk_rows % 8 == 0 else 1

    def put(dst, chunk, src, at):
        for k in range(0, chunk_rows, unit):
            row = aligned(chunk * chunk_rows + k, unit)
            dst[pl.ds(row, unit), :] = src[at + k : at + k + unit, :]

    block = held * chunk_rows
    for src, parity in ((own, core), (other, 1 - core)):
        for h in range(wide // 2):
            put(grads, 2 * h + parity, src, h * chunk_rows)
        for j in range(n):
            for i in range(held):
                chunk = 2 * ((digit ^ j) * held + i) + parity
                at = rows + 8 + 2 * j * block + i * chunk_rows
                put(first, chunk, src, at)
                put(second, chunk, src, at + block)
    gradient = grads[...] / own[rows : rows + 1, :]
    b1 = jnp.full((8, LANES), beta_one[0], f32)
    b2 = jnp.full((8, LANES), beta_two[0], f32)
    count = step[0]
    power1 = jnp.ones((8, LANES), f32)
    power2 = power1
    square1, square2 = b1, b2
    for bit in range(16):
        on = ((count >> bit) & 1) == 1
        power1 = jnp.where(on, power1 * square1, power1)
        power2 = jnp.where(on, power2 * square2, power2)
        square1 = square1 * square1
        square2 = square2 * square2
    b1, b2 = b1[:1], b2[:1]
    m = b1 * first[...] + (1.0 - b1) * gradient
    v = b2 * second[...] + (1.0 - b2) * gradient * gradient
    first[...] = m
    second[...] = v
    moves[...] = (m / (1.0 - power1[:1])) / (jnp.sqrt(v / (1.0 - power2[:1])) + adam_eps)
    for k in range(0, chunk_rows, unit):
        at = aligned(place * chunk_rows + k, unit)
        first_out[k : k + unit, :] = first[pl.ds(at, unit), :]
        second_out[k : k + unit, :] = second[pl.ds(at, unit), :]
    group = LANES // rank
    down_rows = width // group
    up_rows = width // LANES
    for j in range(2):
        spread = jnp.broadcast_to(
            moves[j * down_rows : (j + 1) * down_rows, :][:, None, :], (down_rows, group, LANES)
        ).reshape(width, LANES)
        part = jnp.where(lane_is_feature(width, rank), spread, 0.0)
        move = cdot(lane_is_rank(rank).astype(f32), part, 1, 1, lax.Precision.HIGHEST)
        new_down_t[j] = down_t[j] * (1.0 - rate_first * decay_first) - rate_first * move
        base = 2 * down_rows + j * rank * up_rows
        for cb in range(up_rows):
            cols = slice(cb * LANES, (cb + 1) * LANES)
            new_up[j, :, cols] = up[j, :, cols] * (1.0 - rate_second * decay_second) - (
                rate_second * moves[pl.ds(base + cb, rank, stride=up_rows), :]
            )


def update(beta_one, beta_two, step, own, other, down_t, up, n, held, wide, low):
    n_rows = 2 * down_t.size // LANES
    chunk_rows = n_rows // wide
    smem = pl.BlockSpec(memory_space=pltpu.SMEM)
    vm = pl.BlockSpec(memory_space=VMEM)
    return pl.pallas_call(
        lambda *refs: update_kernel(*refs, n=n, held=held, wide=wide, low=low),
        out_shape=[
            sds(down_t.shape, f32),
            sds(up.shape, f32),
            sds((chunk_rows, LANES), f32),
            sds((chunk_rows, LANES), f32),
        ],
        in_specs=[smem] * 3 + [vm] * 4,
        out_specs=[vm] * 4,
        scratch_shapes=[VMEM((n_rows, LANES), f32)] * 4,
        compiler_params=pltpu.CompilerParams(vmem_limit_bytes=16 << 20),
        name="update",
    )(beta_one, beta_two, step, own, other, down_t, up)


def digit_groups(size, first):
    bits = size.bit_length() - 1
    groups = []
    at = first
    while at < bits:
        n = min(2, bits - at)
        groups.append((at, n))
        at += n
    return groups


def swap_perm(size, mask):
    return [(i, i ^ mask) for i in range(size)]


def exchange(values, axis, size, group):
    low, n = group
    return [values] + [
        lax.ppermute(values, axis, swap_perm(size, j << low)) for j in range(1, 1 << n)
    ]


def tree_sum(parts):
    while len(parts) > 1:
        parts = [parts[i] + parts[i + 1] for i in range(0, len(parts), 2)]
    return parts[0]


def in_order(parts, digit):
    parts = list(parts)
    n = len(parts).bit_length() - 1
    for bit in range(n):
        flip = (digit >> bit) & 1
        parts = [jnp.where(flip == 1, parts[i ^ (1 << bit)], parts[i]) for i in range(len(parts))]
    return parts


def per_device(
    tokens,
    cotangent,
    valid_token_length,
    query_weight_matrix,
    key_weight_matrix,
    value_weight_matrix,
    attention_output_weight,
    inner_ffn_weight,
    outer_ffn_weight,
    query_bias_vector,
    value_bias_vector,
    attention_output_bias,
    hidden_ffn_bias,
    ffn_output_bias,
    layer_norm_gains,
    layer_norm_biases,
    adapter_down_factors,
    adapter_up_factors,
    first_moment_estimate,
    second_moment_estimate,
    first_decay_factor,
    second_decay_factor,
    optimizer_step_number,
):
    dp = lax.axis_size("dp")
    wide = lax.axis_size("wide")
    place = lax.axis_index("wide")
    n_rows = 2 * adapter_down_factors.size // LANES
    chunk_rows = n_rows // wide

    down_t = jnp.swapaxes(adapter_down_factors, 1, 2)
    mixed, token_grad, keep, send = layer(
        valid_token_length,
        tokens,
        cotangent,
        (
            query_weight_matrix,
            key_weight_matrix,
            value_weight_matrix,
            attention_output_weight,
            inner_ffn_weight,
            outer_ffn_weight,
        ),
        (
            query_bias_vector,
            value_bias_vector,
            attention_output_bias,
            hidden_ffn_bias,
            ffn_output_bias,
        ),
        layer_norm_gains,
        layer_norm_biases,
        down_t,
        adapter_up_factors,
        wide,
    )

    grad = keep + lax.ppermute(send, "wide", swap_perm(wide, 1))
    for group in digit_groups(dp, 0):
        grad = tree_sum(exchange(grad, "dp", dp, group))

    first = first_moment_estimate.reshape(chunk_rows, LANES)
    second = second_moment_estimate.reshape(chunk_rows, LANES)
    held = 1
    rows = n_rows // 2 + 8
    groups = digit_groups(wide, 1)
    for i, (low, n) in enumerate(groups):
        pieces = exchange(jnp.concatenate([grad, first, second], axis=0), "wide", wide, (low, n))
        grad = tree_sum([p[:rows] for p in pieces])
        if i + 1 < len(groups):
            block = held * chunk_rows
            pieces = in_order(pieces, place >> low)
            first = jnp.concatenate([p[rows : rows + block] for p in pieces], axis=0)
            second = jnp.concatenate([p[rows + block :] for p in pieces], axis=0)
            held *= len(pieces)
    own = jnp.concatenate([grad] + [p[rows:] for p in pieces], axis=0)
    other = lax.ppermute(own, "wide", swap_perm(wide, 1))
    low, n = groups[-1]
    updated_down_t, updated_up, updated_first, updated_second = update(
        first_decay_factor,
        second_decay_factor,
        optimizer_step_number,
        own,
        other,
        down_t,
        adapter_up_factors,
        1 << n,
        held,
        wide,
        low,
    )
    return (
        mixed,
        token_grad,
        jnp.swapaxes(updated_down_t, 1, 2),
        updated_up,
        updated_first.reshape(-1),
        updated_second.reshape(-1),
    )


def solution(mesh):
    rows = P(("dp", "wide"), None)
    placed = (rows, rows, P(("dp", "wide"))) + (P(),) * 15 + (P("wide"), P("wide")) + (P(),) * 3
    return jax.shard_map(
        per_device,
        mesh=mesh,
        in_specs=placed,
        out_specs=(rows, rows, P(), P(), P("wide"), P("wide")),
        check_vma=False,
    )
```

```python
import jax
import jax.numpy as jnp
from jax import lax
from jax.experimental import pallas as pl
from jax.experimental.pallas import tpu as pltpu
from jax.sharding import PartitionSpec as P

HEADS = 12
HEAD_DIM = 64
LEN_A = 128
LEN_B = 256
LEN_C = 512
BUCKET = 512
LANES = 128

adapter_scale = 2.0
rate_first = 0.005
rate_second = 0.08
decay_first = 0.05
decay_second = 0.01
neg_large = -1e30
norm_eps = 1e-05
adam_eps = 1e-08

f32 = jnp.float32
bf16 = jnp.bfloat16
sds = jax.ShapeDtypeStruct
VMEM = pltpu.VMEM


def cdot(left, right, left_dim, right_dim, precision=None):
    return lax.dot_general(
        left,
        right,
        (((left_dim,), (right_dim,)), ((), ())),
        precision=precision,
        preferred_element_type=f32,
    )


def low_lanes(shape):
    return lax.broadcasted_iota(jnp.int32, shape, 1) < HEAD_DIM


def head_pair_rows(pair, with_ones):
    low = low_lanes(pair.shape)
    zero = jnp.zeros_like(pair)
    first = jnp.where(low, pair, zero)
    second = jnp.where(low, zero, pair)
    if with_ones:
        one = jnp.ones_like(pair)
        first = jnp.concatenate([first, jnp.where(low, one, zero)], axis=1)
        second = jnp.concatenate([second, jnp.where(low, zero, one)], axis=1)
    return jnp.concatenate([first, second], axis=0)


def row_mean(values):
    return jnp.sum(values, axis=1, keepdims=True) * (1.0 / values.shape[1])


def lane_is_rank(rank):
    shape = (rank, LANES)
    return lax.broadcasted_iota(jnp.int32, shape, 1) % rank == lax.broadcasted_iota(
        jnp.int32, shape, 0
    )


def lane_is_feature(rows, rank):
    shape = (rows, LANES)
    return lax.broadcasted_iota(jnp.int32, shape, 0) % (LANES // rank) == (
        lax.broadcasted_iota(jnp.int32, shape, 1) // rank
    )


def flatten_pair(flat, j, spread, up, scale):
    rank, width = up.shape
    group = LANES // rank
    down_rows = width // group
    part = jnp.where(lane_is_feature(width, rank), spread, 0.0)
    flat[j * down_rows : (j + 1) * down_rows, :] = jnp.sum(
        part.reshape(down_rows, group, LANES), axis=1
    )
    up_rows = width // LANES
    base = 2 * down_rows + j * rank * up_rows
    for cb in range(up_rows):
        flat[pl.ds(base + cb, rank, stride=up_rows), :] = (
            scale * up[:, cb * LANES : (cb + 1) * LANES]
        )


def row_moves(wide, chunk_rows):
    unit = 8 if chunk_rows % 8 == 0 else 1
    for h in range(wide // 2):
        for k in range(0, chunk_rows, unit):
            yield h * chunk_rows + k, 2 * h * chunk_rows + k, unit


def aligned(row, unit):
    return pl.multiple_of(row, unit) if unit > 1 else row


def split_half(flat, out, core, wide):
    chunk_rows = flat.shape[0] // wide
    for at, row, unit in row_moves(wide, chunk_rows):
        out[at : at + unit, :] = flat[pl.ds(aligned(row + core * chunk_rows, unit), unit), :]


def layer_kernel(
    lens,
    x_hbm,
    cot_hbm,
    wq_hbm,
    wk_hbm,
    wv_hbm,
    wo_hbm,
    w1_hbm,
    w2_hbm,
    bq,
    bv,
    bo,
    b1,
    b2,
    gains,
    shifts,
    down_t,
    up,
    mixed_hbm,
    midg_hbm,
    dq_hbm,
    dk_hbm,
    dv_hbm,
    wq_out,
    wv_out,
    keep_out,
    send_out,
    x,
    cot,
    wq,
    wk,
    wv,
    wo,
    w1,
    w2,
    acat,
    brep_q,
    brep_v,
    rowv,
    qs,
    ks,
    vs,
    dn,
    probs,
    ctx,
    inv_l,
    dctx,
    act,
    slope,
    mixed,
    midg,
    dq,
    dk,
    dv,
    g_down,
    g_up_q,
    g_up_v,
    flat,
    in_sem,
    w_sem,
    out_sem,
    *,
    wide,
):
    d_model = x.shape[1]
    n_bucket = x.shape[0] // BUCKET
    n_pair = d_model // LANES
    ff = w1.shape[1]
    rank = up.shape[1]
    core = lax.rem(lax.axis_index("wide"), 2)

    def bucket_copy(i, src, dst, sem):
        rows = pl.ds(i * BUCKET, BUCKET)
        return pltpu.make_async_copy(src.at[rows, :], dst.at[rows, :], sem)

    weights = [(wq_hbm, wq), (wk_hbm, wk), (wv_hbm, wv), (wo_hbm, wo), (w1_hbm, w1), (w2_hbm, w2)]
    weight_copies = [pltpu.make_async_copy(s, d, w_sem.at[i]) for i, (s, d) in enumerate(weights)]
    x_copies = [bucket_copy(i, x_hbm, x, in_sem.at[i]) for i in range(n_bucket)]
    cot_copies = [bucket_copy(i, cot_hbm, cot, in_sem.at[n_bucket + i]) for i in range(n_bucket)]
    x_copies[-1].start()
    for c in weight_copies[:4]:
        c.start()
    cot_copies[-1].start()
    for c in weight_copies[4:]:
        c.start()
    for i in reversed(range(n_bucket - 1)):
        x_copies[i].start()
        cot_copies[i].start()

    acat[...] = jnp.concatenate(
        [down_t[0], down_t[1], jnp.zeros((LANES - 2 * rank, d_model), f32)], axis=0
    ).astype(bf16)
    up_q = up[0].astype(bf16).astype(f32) * adapter_scale
    up_v = up[1].astype(bf16).astype(f32) * adapter_scale
    brep_q[...] = jnp.concatenate([up_q] * (LANES // rank), axis=0).astype(bf16)
    brep_v[...] = jnp.concatenate([up_v] * (LANES // rank), axis=0).astype(bf16)
    seq = 0
    row0 = 0
    n_valid = 0
    for length in (LEN_A, LEN_B, LEN_C):
        for s in range(BUCKET // length):
            n = lens[seq]
            n_valid = n_valid + n
            rowv[row0 : row0 + length, :] = (
                lax.broadcasted_iota(jnp.int32, (length, LANES), 0) < n
            ).astype(f32)
            seq += 1
            row0 += length
    g_down[...] = jnp.zeros_like(g_down)
    g_up_q[...] = jnp.zeros_like(g_up_q)
    g_up_v[...] = jnp.zeros_like(g_up_v)

    def pair_at(p, row):
        if isinstance(p, int):
            return slice(p * LANES, (p + 1) * LANES), p * BUCKET + row
        return (
            pl.ds(pl.multiple_of(p * LANES, LANES), LANES),
            pl.multiple_of(p * BUCKET + row, LANES),
        )

    def each_pair(per_step, body):
        if per_step == n_pair:
            for p in range(n_pair):
                body(p, p)
            return

        def step_of(i, carry):
            for j in range(per_step):
                body(i * per_step + j, j)
            return carry

        lax.fori_loop(0, n_pair // per_step, step_of, 0)

    def attend(length, first_seq, p, s):
        rows = slice(s * length, (s + 1) * length)
        cols, prow = pair_at(p, s * length)
        key_rows = head_pair_rows(ks[rows, cols], False)
        val_rows = head_pair_rows(vs[rows, cols], True)
        lane = lax.broadcasted_iota(jnp.int32, (1, length), 1)
        bias = jnp.where(lane < lens[first_seq + s], 0.0, neg_large).astype(f32)
        scores = cdot(qs[rows, cols], key_rows, 1, 1)
        parts = []
        for h in range(2):
            sh = scores[:, h * length : (h + 1) * length] + bias
            parts.append(jnp.exp(sh - jnp.max(sh, axis=1, keepdims=True)).astype(bf16))
        e = jnp.concatenate(parts, axis=1)
        probs[pl.ds(prow, length), : 2 * length] = e
        out = cdot(e, val_rows, 1, 0)
        inv = 1.0 / out[:, LANES:]
        inv_l[rows, cols] = inv
        ctx[rows, cols] = (out[:, :LANES] * inv).astype(bf16)

    def attend_back(length, p, s, values_first):
        rows = slice(s * length, (s + 1) * length)
        cols, prow = pair_at(p, s * length)
        key_rows = head_pair_rows(ks[rows, cols], False)
        val_rows = head_pair_rows(vs[rows, cols], True)
        low = low_lanes((length, LANES))
        dcf = dctx[rows, cols].astype(f32) * inv_l[rows, cols]
        dc = dcf.astype(bf16)
        inner = (-dcf * ctx[rows, cols].astype(f32)).astype(bf16)
        e = probs[pl.ds(prow, length), : 2 * length]

        def value_part():
            rv = cdot(e, dc, 0, 0)
            dv[rows, cols] = jnp.where(low, rv[:length], rv[length:]).astype(bf16)

        if values_first:
            value_part()
        g = cdot(jnp.concatenate([dc, inner], axis=1), val_rows, 1, 1)
        ds = (e.astype(f32) * g).astype(bf16)
        dq[rows, cols] = (cdot(ds, key_rows, 1, 0) * (HEAD_DIM**-0.5)).astype(bf16)
        rk = cdot(ds, qs[rows, cols], 0, 0)
        dk[rows, cols] = jnp.where(low, rk[:length], rk[length:]).astype(bf16)
        if not values_first:
            value_part()

    size = BUCKET // 2
    ahead = (6, 6, 6)
    back = (6, 3, 3)
    step = 256

    def chain(b):
        lrows = [slice(c * size, (c + 1) * size) for c in range(2)]
        grows = [pl.ds(pl.multiple_of(b * BUCKET + c * size, size), size) for c in range(2)]

        def first_norm(c):
            ms = cdot(ctx[lrows[c], :], wo[...], 1, 0) + bo[...][None] + x[grows[c], :].astype(f32)
            xc = ms - row_mean(ms)
            r1 = lax.rsqrt(row_mean(xc * xc) + norm_eps)
            n1 = xc * r1
            return r1, n1, n1 * gains[0:1, :] + shifts[0:1, :]

        def inner_ffn(c, nl):
            for n in range(0, ff, step):
                h = cdot(nl, w1[:, n : n + step], 1, 0) + b1[n : n + step][None]
                cdf = 0.5 + 0.5 * lax.erf(h * (0.5**0.5))
                pdf = jnp.exp(h * h * -0.5) * 0.3989422804014327
                act[lrows[c], n : n + step] = (h * cdf).astype(bf16)
                slope[lrows[c], n : n + step] = (cdf + h * pdf).astype(bf16)

        def second_norm(c, normed):
            fs = cdot(act[lrows[c], :], w2[...], 1, 0) + b2[...][None] + normed
            fc = fs - row_mean(fs)
            r2 = lax.rsqrt(row_mean(fc * fc) + norm_eps)
            n2 = fc * r2
            mixed[lrows[c], :] = (n2 * gains[1:2, :] + shifts[1:2, :]).astype(bf16)
            rv = rowv[grows[c], :]
            e2 = cot[grows[c], :].astype(f32) * jnp.concatenate([rv] * n_pair, axis=1)
            e2 = e2 * gains[1:2, :]
            return r2 * (e2 - row_mean(e2) - n2 * row_mean(e2 * n2))

        def inner_back(c, ol):
            for n in range(0, ff, step):
                da = cdot(ol, w2[n : n + step, :], 1, 1).astype(bf16)
                act[lrows[c], n : n + step] = da * slope[lrows[c], n : n + step]

        def first_back(c, fg, r1, n1):
            e1 = (fg + cdot(act[lrows[c], :], w1[...], 1, 1)) * gains[0:1, :]
            mg = r1 * (e1 - row_mean(e1) - n1 * row_mean(e1 * n1))
            low = mg.astype(bf16)
            midg[lrows[c], :] = low
            dctx[lrows[c], :] = cdot(low, wo[...], 1, 1).astype(bf16)

        r1_a, n1_a, normed_a = first_norm(0)
        r1_b, n1_b, normed_b = first_norm(1)
        inner_ffn(0, normed_a.astype(bf16))
        grad_a = second_norm(0, normed_a)
        inner_ffn(1, normed_b.astype(bf16))
        inner_back(0, grad_a.astype(bf16))
        grad_b = second_norm(1, normed_b)
        first_back(0, grad_a, r1_a, n1_a)
        inner_back(1, grad_b.astype(bf16))
        first_back(1, grad_b, r1_b, n1_b)

    outs = [(mixed, mixed_hbm), (midg, midg_hbm), (dq, dq_hbm), (dk, dk_hbm), (dv, dv_hbm)]
    folded = [(wq, wq_out), (wv, wv_out)]
    folded_copies = [
        pltpu.make_async_copy(s, d, out_sem.at[len(outs) + i]) for i, (s, d) in enumerate(folded)
    ]

    def out_copy(i, b):
        rows = pl.ds(pl.multiple_of(b * BUCKET, BUCKET), BUCKET)
        src, dst = outs[i]
        return pltpu.make_async_copy(src, dst.at[rows, :], out_sem.at[i])

    def out_free(which, b):
        @pl.when(b < n_bucket - 1)
        def _():
            for i in which:
                out_copy(i, b + 1).wait()

    def bucket(step_b, carry):
        b = n_bucket - 1 - step_b
        rows = pl.ds(pl.multiple_of(b * BUCKET, BUCKET), BUCKET)

        def wait_bucket(src, dst, base):
            pltpu.make_async_copy(src.at[rows, :], dst.at[rows, :], in_sem.at[base + b]).wait()

        wait_bucket(x_hbm, x, 0)

        @pl.when(step_b == 0)
        def _():
            for i, (w, low, high) in enumerate(((wq, down_t[0], up_q), (wk, None, None), (wv, down_t[1], up_v))):
                weight_copies[i].wait()
                if low is not None:
                    w[...] = (
                        w[...].astype(f32) + cdot(low.astype(bf16), high.astype(bf16), 0, 0)
                    ).astype(bf16)
            for c in folded_copies:
                c.start()

        xb = x[rows, :]
        dnb = cdot(xb, acat[...], 1, 1).astype(bf16)
        dn[...] = dnb
        qs[...] = (cdot(xb, wq[...], 1, 0) + bq[...][None]).astype(bf16) * jnp.asarray(
            HEAD_DIM**-0.5, bf16
        )
        ks[...] = cdot(xb, wk[...], 1, 0).astype(bf16)
        vs[...] = (cdot(xb, wv[...], 1, 0) + bv[...][None]).astype(bf16)

        first = 0
        for i, length in enumerate((LEN_A, LEN_B, LEN_C)):
            count = BUCKET // length

            @pl.when(b == i)
            def _(i=i, length=length, first=first, count=count):
                def both(p, place):
                    for s in range(count):
                        attend(length, first, p, s)

                each_pair(ahead[i], both)

            first += count

        wait_bucket(cot_hbm, cot, n_bucket)

        @pl.when(step_b == 0)
        def _():
            for c in weight_copies[3:]:
                c.wait()

        out_free((0, 1), b)

        chain(b)
        for i in (0, 1):
            out_copy(i, b).start()
        out_free((2, 3, 4), b)

        for i, length in enumerate((LEN_A, LEN_B, LEN_C)):
            count = BUCKET // length

            @pl.when(b == i)
            def _(i=i, length=length, count=count):
                def both(p, place):
                    for s in range(count):
                        attend_back(length, p, s, (place * count + s) % 2 == 1)

                each_pair(back[i], both)

        for i in (2, 3, 4):
            out_copy(i, b).start()
        dqb = dq[...]
        dvb = dv[...]
        dgb = jnp.concatenate(
            [cdot(dqb, brep_q[...], 1, 1).astype(bf16), cdot(dvb, brep_v[...], 1, 1).astype(bf16)],
            axis=1,
        )
        g_down[...] += cdot(x[rows, :], dgb, 0, 0)
        dnb2 = dn[...]
        g_up_q[...] += cdot(dnb2, dqb, 0, 0)
        g_up_v[...] += cdot(dnb2, dvb, 0, 0)
        return carry

    lax.fori_loop(0, n_bucket, bucket, 0)

    for j, src in enumerate((g_up_q, g_up_v)):
        flatten_pair(
            flat,
            j,
            g_down[:, j * LANES : (j + 1) * LANES],
            src[j * rank : (j + 1) * rank, :],
            adapter_scale,
        )
    n_rows = flat.shape[0]
    split_half(flat, keep_out, core, wide)
    split_half(flat, send_out, 1 - core, wide)
    total = jnp.full((8, LANES), n_valid, jnp.int32).astype(f32)
    keep_out[n_rows // 2 :, :] = total
    send_out[n_rows // 2 :, :] = total
    for i in range(len(outs)):
        out_copy(i, 0).wait()
    for c in folded_copies:
        c.wait()


def layer(lens, x, cot, ws, vecs, gains, shifts, down_t, up, wide):
    t, d = x.shape
    ff = ws[4].shape[1]
    rank = up.shape[1]
    n_rows = 2 * down_t.size // LANES
    n_bucket = t // BUCKET
    any_spec = pl.BlockSpec(memory_space=pl.ANY)
    vm = pl.BlockSpec(memory_space=VMEM)
    ops = [lens, x, cot, *ws, *vecs, gains, shifts, down_t, up]
    in_specs = (
        [pl.BlockSpec(memory_space=pltpu.SMEM)] + [any_spec] * 8 + [vm] * (len(vecs) + 4)
    )
    out_shape = [
        sds((t, d), bf16),
        sds((t, d), bf16),
        sds((t, d), bf16),
        sds((t, d), bf16),
        sds((t, d), bf16),
        sds((d, d), bf16),
        sds((d, d), bf16),
        sds((n_rows // 2 + 8, LANES), f32),
        sds((n_rows // 2 + 8, LANES), f32),
    ]
    dma = pltpu.SemaphoreType.DMA
    scratch = [
        VMEM((t, d), bf16),
        VMEM((t, d), bf16),
        VMEM((d, d), bf16),
        VMEM((d, d), bf16),
        VMEM((d, d), bf16),
        VMEM((d, d), bf16),
        VMEM((d, ff), bf16),
        VMEM((ff, d), bf16),
        VMEM((LANES, d), bf16),
        VMEM((LANES, d), bf16),
        VMEM((LANES, d), bf16),
        VMEM((t, LANES), f32),
        VMEM((BUCKET, d), bf16),
        VMEM((BUCKET, d), bf16),
        VMEM((BUCKET, d), bf16),
        VMEM((BUCKET, LANES), bf16),
        VMEM((d // LANES * BUCKET, 2 * LEN_C), bf16),
        VMEM((BUCKET, d), bf16),
        VMEM((BUCKET, d), f32),
        VMEM((BUCKET, d), bf16),
        VMEM((BUCKET, ff), bf16),
        VMEM((BUCKET, ff), bf16),
        VMEM((BUCKET, d), bf16),
        VMEM((BUCKET, d), bf16),
        VMEM((BUCKET, d), bf16),
        VMEM((BUCKET, d), bf16),
        VMEM((BUCKET, d), bf16),
        VMEM((d, 2 * LANES), f32),
        VMEM((LANES, d), f32),
        VMEM((LANES, d), f32),
        VMEM((n_rows, LANES), f32),
        dma((2 * n_bucket,)),
        dma((6,)),
        dma((7,)),
    ]
    body = lambda *refs: layer_kernel(*refs, wide=wide)
    return pl.pallas_call(
        body,
        out_shape=out_shape,
        in_specs=in_specs,
        out_specs=[any_spec] * 7 + [vm] * 2,
        scratch_shapes=scratch,
        compiler_params=pltpu.CompilerParams(vmem_limit_bytes=63 << 20),
        name="layer",
    )(*ops)


def token_kernel(*refs, first_row):
    mg_hbm, dq_hbm, dk_hbm, dv_hbm, wq_hbm, wk_hbm, wv_hbm, out_hbm = refs[-16:-8]
    mg, grads, weights, acc, out, g_sem, w_sem, m_sem = refs[-8:]
    rows = mg.shape[0]
    chunk = rows // 2
    whole = slice(first_row, first_row + rows)
    for i, (d_hbm, w_hbm) in enumerate(((dq_hbm, wq_hbm), (dk_hbm, wk_hbm), (dv_hbm, wv_hbm))):
        pltpu.make_async_copy(w_hbm, weights.at[i], w_sem.at[i]).start()
        pltpu.make_async_copy(d_hbm.at[whole, :], grads.at[i], g_sem.at[i]).start()
    mid = pltpu.make_async_copy(mg_hbm.at[whole, :], mg, m_sem.at[0])
    mid.start()

    def side(i, carry):
        pltpu.make_async_copy(wq_hbm, weights.at[i], w_sem.at[i]).wait()
        pltpu.make_async_copy(dq_hbm.at[whole, :], grads.at[i], g_sem.at[i]).wait()
        for c in range(2):
            local = slice(c * chunk, (c + 1) * chunk)
            part = cdot(grads[i, local, :], weights[i], 1, 1)
            acc[local, :] = jnp.where(i == 0, part, acc[local, :] + part)
        return carry

    lax.fori_loop(0, 3, side, 0)
    mid.wait()
    writes = []
    for c in range(2):
        local = slice(c * chunk, (c + 1) * chunk)
        out[local, :] = (acc[local, :] + mg[local, :].astype(f32)).astype(bf16)
        at = slice(first_row + c * chunk, first_row + (c + 1) * chunk)
        writes.append(
            pltpu.make_async_copy(out.at[local, :], out_hbm.at[at, :], m_sem.at[1 + c])
        )
        writes[-1].start()
    for w in writes:
        w.wait()


def token_gradient(prev, mg, dq, dk, dv, wq, wk, wv, first_row, rows):
    t, d = mg.shape
    any_spec = pl.BlockSpec(memory_space=pl.ANY)
    args = (mg, dq, dk, dv, wq, wk, wv)
    aliases = {}
    if prev is not None:
        args = (prev,) + args
        aliases = {0: 0}
    dma = pltpu.SemaphoreType.DMA
    return pl.pallas_call(
        lambda *refs: token_kernel(*refs, first_row=first_row),
        out_shape=sds((t, d), bf16),
        in_specs=[any_spec] * len(args),
        out_specs=any_spec,
        scratch_shapes=[
            VMEM((rows, d), bf16),
            VMEM((3, rows, d), bf16),
            VMEM((3, d, d), bf16),
            VMEM((rows, d), f32),
            VMEM((rows, d), bf16),
            dma((3,)),
            dma((3,)),
            dma((3,)),
        ],
        input_output_aliases=aliases,
        compiler_params=pltpu.CompilerParams(vmem_limit_bytes=60 << 20),
        cost_estimate=pl.CostEstimate(
            flops=6 * rows * d * d, bytes_accessed=10 * rows * d, transcendentals=0
        ),
        name="token_gradient",
    )(*args)


def update_kernel(
    beta_one, beta_two, step, own, other, down_t, up, new_down_t, new_up, first_out, second_out, *scratch, n, held, wide, low
):
    grads, first, second, moves = scratch
    rank, width = up.shape[1:]
    n_rows = grads.shape[0]
    rows = n_rows // 2
    chunk_rows = n_rows // wide
    place = lax.axis_index("wide")
    core = lax.rem(place, 2)
    digit = (place >> low) % n
    unit = 8 if chunk_rows % 8 == 0 else 1

    def put(dst, chunk, src, at):
        for k in range(0, chunk_rows, unit):
            row = aligned(chunk * chunk_rows + k, unit)
            dst[pl.ds(row, unit), :] = src[at + k : at + k + unit, :]

    block = held * chunk_rows
    for src, parity in ((own, core), (other, 1 - core)):
        for h in range(wide // 2):
            put(grads, 2 * h + parity, src, h * chunk_rows)
        for j in range(n):
            for i in range(held):
                chunk = 2 * ((digit ^ j) * held + i) + parity
                at = rows + 8 + 2 * j * block + i * chunk_rows
                put(first, chunk, src, at)
                put(second, chunk, src, at + block)
    gradient = grads[...] / own[rows : rows + 1, :]
    b1 = jnp.full((8, LANES), beta_one[0], f32)
    b2 = jnp.full((8, LANES), beta_two[0], f32)
    count = step[0]
    power1 = jnp.ones((8, LANES), f32)
    power2 = power1
    square1, square2 = b1, b2
    for bit in range(16):
        on = ((count >> bit) & 1) == 1
        power1 = jnp.where(on, power1 * square1, power1)
        power2 = jnp.where(on, power2 * square2, power2)
        square1 = square1 * square1
        square2 = square2 * square2
    b1, b2 = b1[:1], b2[:1]
    m = b1 * first[...] + (1.0 - b1) * gradient
    v = b2 * second[...] + (1.0 - b2) * gradient * gradient
    first[...] = m
    second[...] = v
    moves[...] = (m / (1.0 - power1[:1])) / (jnp.sqrt(v / (1.0 - power2[:1])) + adam_eps)
    for k in range(0, chunk_rows, unit):
        at = aligned(place * chunk_rows + k, unit)
        first_out[k : k + unit, :] = first[pl.ds(at, unit), :]
        second_out[k : k + unit, :] = second[pl.ds(at, unit), :]
    group = LANES // rank
    down_rows = width // group
    up_rows = width // LANES
    for j in range(2):
        spread = jnp.broadcast_to(
            moves[j * down_rows : (j + 1) * down_rows, :][:, None, :], (down_rows, group, LANES)
        ).reshape(width, LANES)
        part = jnp.where(lane_is_feature(width, rank), spread, 0.0)
        move = cdot(lane_is_rank(rank).astype(f32), part, 1, 1, lax.Precision.HIGHEST)
        new_down_t[j] = down_t[j] * (1.0 - rate_first * decay_first) - rate_first * move
        base = 2 * down_rows + j * rank * up_rows
        for cb in range(up_rows):
            cols = slice(cb * LANES, (cb + 1) * LANES)
            new_up[j, :, cols] = up[j, :, cols] * (1.0 - rate_second * decay_second) - (
                rate_second * moves[pl.ds(base + cb, rank, stride=up_rows), :]
            )


def update(beta_one, beta_two, step, own, other, down_t, up, n, held, wide, low):
    n_rows = 2 * down_t.size // LANES
    chunk_rows = n_rows // wide
    smem = pl.BlockSpec(memory_space=pltpu.SMEM)
    vm = pl.BlockSpec(memory_space=VMEM)
    return pl.pallas_call(
        lambda *refs: update_kernel(*refs, n=n, held=held, wide=wide, low=low),
        out_shape=[
            sds(down_t.shape, f32),
            sds(up.shape, f32),
            sds((chunk_rows, LANES), f32),
            sds((chunk_rows, LANES), f32),
        ],
        in_specs=[smem] * 3 + [vm] * 4,
        out_specs=[vm] * 4,
        scratch_shapes=[VMEM((n_rows, LANES), f32)] * 4,
        compiler_params=pltpu.CompilerParams(vmem_limit_bytes=16 << 20),
        name="update",
    )(beta_one, beta_two, step, own, other, down_t, up)


def digit_groups(size, first):
    bits = size.bit_length() - 1
    groups = []
    at = first
    while at < bits:
        n = min(2, bits - at)
        groups.append((at, n))
        at += n
    return groups


def swap_perm(size, mask):
    return [(i, i ^ mask) for i in range(size)]


def exchange(values, axis, size, group):
    low, n = group
    return [values] + [
        lax.ppermute(values, axis, swap_perm(size, j << low)) for j in range(1, 1 << n)
    ]


def tree_sum(parts):
    while len(parts) > 1:
        parts = [parts[i] + parts[i + 1] for i in range(0, len(parts), 2)]
    return parts[0]


def in_order(parts, digit):
    parts = list(parts)
    n = len(parts).bit_length() - 1
    for bit in range(n):
        flip = (digit >> bit) & 1
        parts = [jnp.where(flip == 1, parts[i ^ (1 << bit)], parts[i]) for i in range(len(parts))]
    return parts


def per_device(
    tokens,
    cotangent,
    valid_token_length,
    query_weight_matrix,
    key_weight_matrix,
    value_weight_matrix,
    attention_output_weight,
    inner_ffn_weight,
    outer_ffn_weight,
    query_bias_vector,
    value_bias_vector,
    attention_output_bias,
    hidden_ffn_bias,
    ffn_output_bias,
    layer_norm_gains,
    layer_norm_biases,
    adapter_down_factors,
    adapter_up_factors,
    first_moment_estimate,
    second_moment_estimate,
    first_decay_factor,
    second_decay_factor,
    optimizer_step_number,
):
    dp = lax.axis_size("dp")
    wide = lax.axis_size("wide")
    place = lax.axis_index("wide")
    n_rows = 2 * adapter_down_factors.size // LANES
    chunk_rows = n_rows // wide

    down_t = jnp.swapaxes(adapter_down_factors, 1, 2)
    mixed, midg, dq, dk, dv, folded_q, folded_v, keep, send = layer(
        valid_token_length,
        tokens,
        cotangent,
        (
            query_weight_matrix,
            key_weight_matrix,
            value_weight_matrix,
            attention_output_weight,
            inner_ffn_weight,
            outer_ffn_weight,
        ),
        (
            query_bias_vector,
            value_bias_vector,
            attention_output_bias,
            hidden_ffn_bias,
            ffn_output_bias,
        ),
        layer_norm_gains,
        layer_norm_biases,
        down_t,
        adapter_up_factors,
        wide,
    )

    def token_part(prev, after, first_row, rows):
        held_back, _ = lax.optimization_barrier((midg, after))
        return token_gradient(
            prev, held_back, dq, dk, dv, folded_q, key_weight_matrix, folded_v, first_row, rows
        )

    n_tok = tokens.shape[0]
    grad = keep + lax.ppermute(send, "wide", swap_perm(wide, 1))
    token_grad = token_part(None, grad, 0, n_tok // 2)
    for i, group in enumerate(digit_groups(dp, 0)):
        pieces = exchange(grad, "dp", dp, group)
        if i == 0:
            pieces, token_grad = lax.optimization_barrier((pieces, token_grad))
        grad = tree_sum(pieces)
    token_grad = token_part(token_grad, grad, n_tok // 2, n_tok // 2)

    first = first_moment_estimate.reshape(chunk_rows, LANES)
    second = second_moment_estimate.reshape(chunk_rows, LANES)
    held = 1
    rows = n_rows // 2 + 8
    groups = digit_groups(wide, 1)
    for i, (low, n) in enumerate(groups):
        pieces = exchange(jnp.concatenate([grad, first, second], axis=0), "wide", wide, (low, n))
        if i == 0:
            pieces, token_grad = lax.optimization_barrier((pieces, token_grad))
        grad = tree_sum([p[:rows] for p in pieces])
        if i + 1 < len(groups):
            block = held * chunk_rows
            pieces = in_order(pieces, place >> low)
            first = jnp.concatenate([p[rows : rows + block] for p in pieces], axis=0)
            second = jnp.concatenate([p[rows + block :] for p in pieces], axis=0)
            held *= len(pieces)
    own = jnp.concatenate([grad] + [p[rows:] for p in pieces], axis=0)
    other = lax.ppermute(own, "wide", swap_perm(wide, 1))
    low, n = groups[-1]
    updated_down_t, updated_up, updated_first, updated_second = update(
        first_decay_factor,
        second_decay_factor,
        optimizer_step_number,
        own,
        other,
        down_t,
        adapter_up_factors,
        1 << n,
        held,
        wide,
        low,
    )
    return (
        mixed,
        token_grad,
        jnp.swapaxes(updated_down_t, 1, 2),
        updated_up,
        updated_first.reshape(-1),
        updated_second.reshape(-1),
    )


def solution(mesh):
    rows = P(("dp", "wide"), None)
    placed = (rows, rows, P(("dp", "wide"))) + (P(),) * 15 + (P("wide"), P("wide")) + (P(),) * 3
    return jax.shard_map(
        per_device,
        mesh=mesh,
        in_specs=placed,
        out_specs=(rows, rows, P(), P(), P("wide"), P("wide")),
        check_vma=False,
    )
```

```python
import jax
import jax.numpy as jnp
from jax import lax
from jax.experimental import pallas as pl
from jax.experimental.pallas import tpu as pltpu
from jax.sharding import PartitionSpec as P

HEADS = 12
HEAD_DIM = 64
LEN_A = 128
LEN_B = 256
LEN_C = 512
BUCKET = 512
LANES = 128

adapter_scale = 2.0
rate_first = 0.005
rate_second = 0.08
decay_first = 0.05
decay_second = 0.01
neg_large = -1e30
norm_eps = 1e-05
adam_eps = 1e-08

f32 = jnp.float32
bf16 = jnp.bfloat16
sds = jax.ShapeDtypeStruct
VMEM = pltpu.VMEM


def cdot(left, right, left_dim, right_dim, precision=None):
    return lax.dot_general(
        left,
        right,
        (((left_dim,), (right_dim,)), ((), ())),
        precision=precision,
        preferred_element_type=f32,
    )


def low_lanes(shape):
    return lax.broadcasted_iota(jnp.int32, shape, 1) < HEAD_DIM


def head_pair_rows(pair, with_ones):
    low = low_lanes(pair.shape)
    zero = jnp.zeros_like(pair)
    first = jnp.where(low, pair, zero)
    second = jnp.where(low, zero, pair)
    if with_ones:
        one = jnp.ones_like(pair)
        first = jnp.concatenate([first, jnp.where(low, one, zero)], axis=1)
        second = jnp.concatenate([second, jnp.where(low, zero, one)], axis=1)
    return jnp.concatenate([first, second], axis=0)


def row_mean(values):
    return jnp.sum(values, axis=1, keepdims=True) * (1.0 / values.shape[1])


def lane_is_rank(rank):
    shape = (rank, LANES)
    return lax.broadcasted_iota(jnp.int32, shape, 1) % rank == lax.broadcasted_iota(
        jnp.int32, shape, 0
    )


def lane_is_feature(rows, rank):
    shape = (rows, LANES)
    return lax.broadcasted_iota(jnp.int32, shape, 0) % (LANES // rank) == (
        lax.broadcasted_iota(jnp.int32, shape, 1) // rank
    )


def flatten_pair(flat, j, spread, up):
    rank, width = up.shape
    group = LANES // rank
    down_rows = width // group
    part = jnp.where(lane_is_feature(width, rank), spread, 0.0)
    flat[j * down_rows : (j + 1) * down_rows, :] = jnp.sum(
        part.reshape(down_rows, group, LANES), axis=1
    )
    up_rows = width // LANES
    base = 2 * down_rows + j * rank * up_rows
    for cb in range(up_rows):
        flat[pl.ds(base + cb, rank, stride=up_rows), :] = up[:, cb * LANES : (cb + 1) * LANES]


def row_moves(wide, chunk_rows):
    unit = 8 if chunk_rows % 8 == 0 else 1
    for h in range(wide // 2):
        for k in range(0, chunk_rows, unit):
            yield h * chunk_rows + k, 2 * h * chunk_rows + k, unit


def aligned(row, unit):
    return pl.multiple_of(row, unit) if unit > 1 else row


def split_half(flat, out, core, wide):
    chunk_rows = flat.shape[0] // wide
    for at, row, unit in row_moves(wide, chunk_rows):
        out[at : at + unit, :] = flat[pl.ds(aligned(row + core * chunk_rows, unit), unit), :]


def layer_kernel(
    lens,
    x_hbm,
    cot_hbm,
    wq_hbm,
    wk_hbm,
    wv_hbm,
    wo_hbm,
    w1_hbm,
    w2_hbm,
    bq,
    bv,
    bo,
    b1,
    b2,
    gains,
    shifts,
    down_t,
    up,
    mixed_hbm,
    midg_hbm,
    dq_hbm,
    dk_hbm,
    dv_hbm,
    wq_out,
    wv_out,
    keep_out,
    send_out,
    x,
    cot,
    wq,
    wk,
    wv,
    wo,
    w1,
    w2,
    acat,
    brep_q,
    brep_v,
    rowv,
    qs,
    ks,
    vs,
    dn,
    probs,
    ctx,
    inv_l,
    dctx,
    act,
    slope,
    mixed,
    midg,
    dq,
    dk,
    dv,
    g_down,
    g_up_q,
    g_up_v,
    flat,
    in_sem,
    w_sem,
    out_sem,
    *,
    wide,
):
    d_model = x.shape[1]
    n_bucket = x.shape[0] // BUCKET
    n_pair = d_model // LANES
    ff = w1.shape[1]
    rank = up.shape[1]
    core = lax.rem(lax.axis_index("wide"), 2)

    def bucket_copy(i, src, dst, sem):
        rows = pl.ds(i * BUCKET, BUCKET)
        return pltpu.make_async_copy(src.at[rows, :], dst.at[rows, :], sem)

    weights = [(wq_hbm, wq), (wk_hbm, wk), (wv_hbm, wv), (wo_hbm, wo), (w1_hbm, w1), (w2_hbm, w2)]
    weight_copies = [pltpu.make_async_copy(s, d, w_sem.at[i]) for i, (s, d) in enumerate(weights)]
    x_copies = [bucket_copy(i, x_hbm, x, in_sem.at[i]) for i in range(n_bucket)]
    cot_copies = [bucket_copy(i, cot_hbm, cot, in_sem.at[n_bucket + i]) for i in range(n_bucket)]
    x_copies[-1].start()
    for c in weight_copies[:4]:
        c.start()
    cot_copies[-1].start()
    for c in weight_copies[4:]:
        c.start()
    for i in reversed(range(n_bucket - 1)):
        x_copies[i].start()
        cot_copies[i].start()

    acat[...] = jnp.concatenate(
        [down_t[0], down_t[1], jnp.zeros((LANES - 2 * rank, d_model), f32)], axis=0
    ).astype(bf16)
    up_q = up[0].astype(bf16).astype(f32) * adapter_scale
    up_v = up[1].astype(bf16).astype(f32) * adapter_scale
    brep_q[...] = jnp.concatenate([up_q] * (LANES // rank), axis=0).astype(bf16)
    brep_v[...] = jnp.concatenate([up_v] * (LANES // rank), axis=0).astype(bf16)
    seq = 0
    row0 = 0
    n_valid = 0
    for length in (LEN_A, LEN_B, LEN_C):
        for s in range(BUCKET // length):
            n = lens[seq]
            n_valid = n_valid + n
            rowv[row0 : row0 + length, :] = (
                lax.broadcasted_iota(jnp.int32, (length, LANES), 0) < n
            ).astype(f32)
            seq += 1
            row0 += length
    g_down[...] = jnp.zeros_like(g_down)
    g_up_q[...] = jnp.zeros_like(g_up_q)
    g_up_v[...] = jnp.zeros_like(g_up_v)

    def pair_at(p, row):
        if isinstance(p, int):
            return slice(p * LANES, (p + 1) * LANES), p * BUCKET + row
        return (
            pl.ds(pl.multiple_of(p * LANES, LANES), LANES),
            pl.multiple_of(p * BUCKET + row, LANES),
        )

    def each_pair(per_step, body):
        if per_step == n_pair:
            for p in range(n_pair):
                body(p, p)
            return

        def step_of(i, carry):
            for j in range(per_step):
                body(i * per_step + j, j)
            return carry

        lax.fori_loop(0, n_pair // per_step, step_of, 0)

    def attend(length, first_seq, p, s):
        rows = slice(s * length, (s + 1) * length)
        cols, prow = pair_at(p, s * length)
        key_rows = head_pair_rows(ks[rows, cols], False)
        val_rows = head_pair_rows(vs[rows, cols], True)
        lane = lax.broadcasted_iota(jnp.int32, (1, length), 1)
        bias = jnp.where(lane < lens[first_seq + s], 0.0, neg_large).astype(f32)
        scores = cdot(qs[rows, cols], key_rows, 1, 1)
        parts = []
        for h in range(2):
            sh = scores[:, h * length : (h + 1) * length] + bias
            parts.append(jnp.exp(sh - jnp.max(sh, axis=1, keepdims=True)).astype(bf16))
        e = jnp.concatenate(parts, axis=1)
        probs[pl.ds(prow, length), : 2 * length] = e
        out = cdot(e, val_rows, 1, 0)
        inv = 1.0 / out[:, LANES:]
        inv_l[rows, cols] = inv
        ctx[rows, cols] = (out[:, :LANES] * inv).astype(bf16)

    def attend_back(length, p, s, values_first):
        rows = slice(s * length, (s + 1) * length)
        cols, prow = pair_at(p, s * length)
        key_rows = head_pair_rows(ks[rows, cols], False)
        val_rows = head_pair_rows(vs[rows, cols], True)
        low = low_lanes((length, LANES))
        dcf = dctx[rows, cols].astype(f32) * inv_l[rows, cols]
        dc = dcf.astype(bf16)
        inner = (-dcf * ctx[rows, cols].astype(f32)).astype(bf16)
        e = probs[pl.ds(prow, length), : 2 * length]

        def value_part():
            rv = cdot(e, dc, 0, 0)
            dv[rows, cols] = jnp.where(low, rv[:length], rv[length:]).astype(bf16)

        if values_first:
            value_part()
        g = cdot(jnp.concatenate([dc, inner], axis=1), val_rows, 1, 1)
        ds = (e.astype(f32) * g).astype(bf16)
        dq[rows, cols] = (cdot(ds, key_rows, 1, 0) * (HEAD_DIM**-0.5)).astype(bf16)
        rk = cdot(ds, qs[rows, cols], 0, 0)
        dk[rows, cols] = jnp.where(low, rk[:length], rk[length:]).astype(bf16)
        if not values_first:
            value_part()

    size = BUCKET // 2
    ahead = (6, 6, 6)
    back = (6, 3, 3)
    step = 256

    def chain(b):
        lrows = [slice(c * size, (c + 1) * size) for c in range(2)]
        grows = [pl.ds(pl.multiple_of(b * BUCKET + c * size, size), size) for c in range(2)]

        def first_norm(c):
            ms = cdot(ctx[lrows[c], :], wo[...], 1, 0) + bo[...][None] + x[grows[c], :].astype(f32)
            xc = ms - row_mean(ms)
            r1 = lax.rsqrt(row_mean(xc * xc) + norm_eps)
            n1 = xc * r1
            return r1, n1, n1 * gains[0:1, :] + shifts[0:1, :]

        def inner_ffn(c, nl):
            for n in range(0, ff, step):
                h = cdot(nl, w1[:, n : n + step], 1, 0) + b1[n : n + step][None]
                cdf = 0.5 + 0.5 * lax.erf(h * (0.5**0.5))
                pdf = jnp.exp(h * h * -0.5) * 0.3989422804014327
                act[lrows[c], n : n + step] = (h * cdf).astype(bf16)
                slope[lrows[c], n : n + step] = (cdf + h * pdf).astype(bf16)

        def second_norm(c, normed):
            fs = cdot(act[lrows[c], :], w2[...], 1, 0) + b2[...][None] + normed
            fc = fs - row_mean(fs)
            r2 = lax.rsqrt(row_mean(fc * fc) + norm_eps)
            n2 = fc * r2
            mixed[lrows[c], :] = (n2 * gains[1:2, :] + shifts[1:2, :]).astype(bf16)
            rv = rowv[grows[c], :]
            e2 = cot[grows[c], :].astype(f32) * jnp.concatenate([rv] * n_pair, axis=1)
            e2 = e2 * gains[1:2, :]
            return r2 * (e2 - row_mean(e2) - n2 * row_mean(e2 * n2))

        def inner_back(c, ol):
            for n in range(0, ff, step):
                da = cdot(ol, w2[n : n + step, :], 1, 1).astype(bf16)
                act[lrows[c], n : n + step] = da * slope[lrows[c], n : n + step]

        def first_back(c, fg, r1, n1):
            e1 = (fg + cdot(act[lrows[c], :], w1[...], 1, 1)) * gains[0:1, :]
            mg = r1 * (e1 - row_mean(e1) - n1 * row_mean(e1 * n1))
            low = mg.astype(bf16)
            midg[lrows[c], :] = low
            dctx[lrows[c], :] = cdot(low, wo[...], 1, 1).astype(bf16)

        r1_a, n1_a, normed_a = first_norm(0)
        r1_b, n1_b, normed_b = first_norm(1)
        inner_ffn(0, normed_a.astype(bf16))
        grad_a = second_norm(0, normed_a)
        inner_ffn(1, normed_b.astype(bf16))
        inner_back(0, grad_a.astype(bf16))
        grad_b = second_norm(1, normed_b)
        first_back(0, grad_a, r1_a, n1_a)
        inner_back(1, grad_b.astype(bf16))
        first_back(1, grad_b, r1_b, n1_b)

    outs = [(mixed, mixed_hbm), (midg, midg_hbm), (dq, dq_hbm), (dk, dk_hbm), (dv, dv_hbm)]
    folded = [(wq, wq_out), (wv, wv_out)]
    folded_copies = [
        pltpu.make_async_copy(s, d, out_sem.at[len(outs) + i]) for i, (s, d) in enumerate(folded)
    ]

    def out_copy(i, b):
        rows = pl.ds(pl.multiple_of(b * BUCKET, BUCKET), BUCKET)
        src, dst = outs[i]
        return pltpu.make_async_copy(src, dst.at[rows, :], out_sem.at[i])

    def out_free(which, b):
        @pl.when(b < n_bucket - 1)
        def _():
            for i in which:
                out_copy(i, b + 1).wait()

    def bucket(step_b, carry):
        b = n_bucket - 1 - step_b
        rows = pl.ds(pl.multiple_of(b * BUCKET, BUCKET), BUCKET)

        def wait_bucket(src, dst, base):
            pltpu.make_async_copy(src.at[rows, :], dst.at[rows, :], in_sem.at[base + b]).wait()

        wait_bucket(x_hbm, x, 0)

        @pl.when(step_b == 0)
        def _():
            for i, (w, low, high) in enumerate(((wq, down_t[0], up_q), (wk, None, None), (wv, down_t[1], up_v))):
                weight_copies[i].wait()
                if low is not None:
                    w[...] = (
                        w[...].astype(f32) + cdot(low.astype(bf16), high.astype(bf16), 0, 0)
                    ).astype(bf16)
            for c in folded_copies:
                c.start()

        xb = x[rows, :]
        dnb = cdot(xb, acat[...], 1, 1).astype(bf16)
        dn[...] = dnb
        qs[...] = (cdot(xb, wq[...], 1, 0) + bq[...][None]).astype(bf16) * jnp.asarray(
            HEAD_DIM**-0.5, bf16
        )
        ks[...] = cdot(xb, wk[...], 1, 0).astype(bf16)
        vs[...] = (cdot(xb, wv[...], 1, 0) + bv[...][None]).astype(bf16)

        first = 0
        for i, length in enumerate((LEN_A, LEN_B, LEN_C)):
            count = BUCKET // length

            @pl.when(b == i)
            def _(i=i, length=length, first=first, count=count):
                def both(p, place):
                    for s in range(count):
                        attend(length, first, p, s)

                each_pair(ahead[i], both)

            first += count

        wait_bucket(cot_hbm, cot, n_bucket)

        @pl.when(step_b == 0)
        def _():
            for c in weight_copies[3:]:
                c.wait()

        out_free((0, 1), b)

        chain(b)
        for i in (0, 1):
            out_copy(i, b).start()
        out_free((2, 3, 4), b)

        for i, length in enumerate((LEN_A, LEN_B, LEN_C)):
            count = BUCKET // length

            @pl.when(b == i)
            def _(i=i, length=length, count=count):
                def both(p, place):
                    for s in range(count):
                        attend_back(length, p, s, (place * count + s) % 2 == 1)

                each_pair(back[i], both)

        for i in (2, 3, 4):
            out_copy(i, b).start()
        dqb = dq[...]
        dvb = dv[...]
        dgb = jnp.concatenate(
            [cdot(dqb, brep_q[...], 1, 1).astype(bf16), cdot(dvb, brep_v[...], 1, 1).astype(bf16)],
            axis=1,
        )
        g_down[...] += cdot(x[rows, :], dgb, 0, 0)
        dnb2 = dn[:, : 2 * rank]
        g_up_q[...] += cdot(dnb2, dqb, 0, 0)
        g_up_v[...] += cdot(dnb2, dvb, 0, 0)
        return carry

    lax.fori_loop(0, n_bucket, bucket, 0)

    for j, src in enumerate((g_up_q, g_up_v)):
        flatten_pair(
            flat,
            j,
            g_down[:, j * LANES : (j + 1) * LANES],
            src[j * rank : (j + 1) * rank, :],
        )
    n_rows = flat.shape[0]
    split_half(flat, keep_out, core, wide)
    split_half(flat, send_out, 1 - core, wide)
    total = jnp.full((8, LANES), n_valid, jnp.int32).astype(f32)
    keep_out[n_rows // 2 :, :] = total
    send_out[n_rows // 2 :, :] = total
    for i in range(len(outs)):
        out_copy(i, 0).wait()
    for c in folded_copies:
        c.wait()


def layer(lens, x, cot, ws, vecs, gains, shifts, down_t, up, wide):
    t, d = x.shape
    ff = ws[4].shape[1]
    rank = up.shape[1]
    n_rows = 2 * down_t.size // LANES
    n_bucket = t // BUCKET
    any_spec = pl.BlockSpec(memory_space=pl.ANY)
    vm = pl.BlockSpec(memory_space=VMEM)
    ops = [lens, x, cot, *ws, *vecs, gains, shifts, down_t, up]
    in_specs = (
        [pl.BlockSpec(memory_space=pltpu.SMEM)] + [any_spec] * 8 + [vm] * (len(vecs) + 4)
    )
    out_shape = [
        sds((t, d), bf16),
        sds((t, d), bf16),
        sds((t, d), bf16),
        sds((t, d), bf16),
        sds((t, d), bf16),
        sds((d, d), bf16),
        sds((d, d), bf16),
        sds((n_rows // 2 + 8, LANES), f32),
        sds((n_rows // 2 + 8, LANES), f32),
    ]
    dma = pltpu.SemaphoreType.DMA
    scratch = [
        VMEM((t, d), bf16),
        VMEM((t, d), bf16),
        VMEM((d, d), bf16),
        VMEM((d, d), bf16),
        VMEM((d, d), bf16),
        VMEM((d, d), bf16),
        VMEM((d, ff), bf16),
        VMEM((ff, d), bf16),
        VMEM((LANES, d), bf16),
        VMEM((LANES, d), bf16),
        VMEM((LANES, d), bf16),
        VMEM((t, LANES), f32),
        VMEM((BUCKET, d), bf16),
        VMEM((BUCKET, d), bf16),
        VMEM((BUCKET, d), bf16),
        VMEM((BUCKET, LANES), bf16),
        VMEM((d // LANES * BUCKET, 2 * LEN_C), bf16),
        VMEM((BUCKET, d), bf16),
        VMEM((BUCKET, d), f32),
        VMEM((BUCKET, d), bf16),
        VMEM((BUCKET, ff), bf16),
        VMEM((BUCKET, ff), bf16),
        VMEM((BUCKET, d), bf16),
        VMEM((BUCKET, d), bf16),
        VMEM((BUCKET, d), bf16),
        VMEM((BUCKET, d), bf16),
        VMEM((BUCKET, d), bf16),
        VMEM((d, 2 * LANES), f32),
        VMEM((2 * rank, d), f32),
        VMEM((2 * rank, d), f32),
        VMEM((n_rows, LANES), f32),
        dma((2 * n_bucket,)),
        dma((6,)),
        dma((7,)),
    ]
    body = lambda *refs: layer_kernel(*refs, wide=wide)
    return pl.pallas_call(
        body,
        out_shape=out_shape,
        in_specs=in_specs,
        out_specs=[any_spec] * 7 + [vm] * 2,
        scratch_shapes=scratch,
        compiler_params=pltpu.CompilerParams(vmem_limit_bytes=63 << 20),
        name="layer",
    )(*ops)


def token_kernel(*refs, first_row):
    mg_hbm, dq_hbm, dk_hbm, dv_hbm, wq_hbm, wk_hbm, wv_hbm, out_hbm = refs[-16:-8]
    mg, grads, weights, acc, out, g_sem, w_sem, m_sem = refs[-8:]
    rows = mg.shape[0]
    chunk = rows // 2
    whole = slice(first_row, first_row + rows)
    for i, (d_hbm, w_hbm) in enumerate(((dq_hbm, wq_hbm), (dk_hbm, wk_hbm), (dv_hbm, wv_hbm))):
        pltpu.make_async_copy(w_hbm, weights.at[i], w_sem.at[i]).start()
        pltpu.make_async_copy(d_hbm.at[whole, :], grads.at[i], g_sem.at[i]).start()
    mid = pltpu.make_async_copy(mg_hbm.at[whole, :], mg, m_sem.at[0])
    mid.start()

    def side(i, carry):
        pltpu.make_async_copy(wq_hbm, weights.at[i], w_sem.at[i]).wait()
        pltpu.make_async_copy(dq_hbm.at[whole, :], grads.at[i], g_sem.at[i]).wait()
        for c in range(2):
            local = slice(c * chunk, (c + 1) * chunk)
            part = cdot(grads[i, local, :], weights[i], 1, 1)
            acc[local, :] = jnp.where(i == 0, part, acc[local, :] + part)
        return carry

    lax.fori_loop(0, 3, side, 0)
    mid.wait()
    writes = []
    for c in range(2):
        local = slice(c * chunk, (c + 1) * chunk)
        out[local, :] = (acc[local, :] + mg[local, :].astype(f32)).astype(bf16)
        at = slice(first_row + c * chunk, first_row + (c + 1) * chunk)
        writes.append(
            pltpu.make_async_copy(out.at[local, :], out_hbm.at[at, :], m_sem.at[1 + c])
        )
        writes[-1].start()
    for w in writes:
        w.wait()


def token_gradient(prev, mg, dq, dk, dv, wq, wk, wv, first_row, rows):
    t, d = mg.shape
    any_spec = pl.BlockSpec(memory_space=pl.ANY)
    args = (mg, dq, dk, dv, wq, wk, wv)
    aliases = {}
    if prev is not None:
        args = (prev,) + args
        aliases = {0: 0}
    dma = pltpu.SemaphoreType.DMA
    return pl.pallas_call(
        lambda *refs: token_kernel(*refs, first_row=first_row),
        out_shape=sds((t, d), bf16),
        in_specs=[any_spec] * len(args),
        out_specs=any_spec,
        scratch_shapes=[
            VMEM((rows, d), bf16),
            VMEM((3, rows, d), bf16),
            VMEM((3, d, d), bf16),
            VMEM((rows, d), f32),
            VMEM((rows, d), bf16),
            dma((3,)),
            dma((3,)),
            dma((3,)),
        ],
        input_output_aliases=aliases,
        compiler_params=pltpu.CompilerParams(vmem_limit_bytes=60 << 20),
        cost_estimate=pl.CostEstimate(
            flops=6 * rows * d * d, bytes_accessed=10 * rows * d, transcendentals=0
        ),
        name="token_gradient",
    )(*args)


def update_kernel(
    beta_one, beta_two, step, own, other, down_t, up, new_down_t, new_up, first_out, second_out, *scratch, n, held, wide, low
):
    grads, first, second, moves = scratch
    rank, width = up.shape[1:]
    n_rows = grads.shape[0]
    rows = n_rows // 2
    chunk_rows = n_rows // wide
    place = lax.axis_index("wide")
    core = lax.rem(place, 2)
    digit = (place >> low) % n
    unit = 8 if chunk_rows % 8 == 0 else 1

    def put(dst, chunk, src, at):
        for k in range(0, chunk_rows, unit):
            row = aligned(chunk * chunk_rows + k, unit)
            dst[pl.ds(row, unit), :] = src[at + k : at + k + unit, :]

    block = held * chunk_rows
    for src, parity in ((own, core), (other, 1 - core)):
        for h in range(wide // 2):
            put(grads, 2 * h + parity, src, h * chunk_rows)
        for j in range(n):
            for i in range(held):
                chunk = 2 * ((digit ^ j) * held + i) + parity
                at = rows + 8 + 2 * j * block + i * chunk_rows
                put(first, chunk, src, at)
                put(second, chunk, src, at + block)
    gradient = grads[...] / own[rows : rows + 1, :]
    b1 = jnp.full((8, LANES), beta_one[0], f32)
    b2 = jnp.full((8, LANES), beta_two[0], f32)
    count = step[0]
    power1 = jnp.ones((8, LANES), f32)
    power2 = power1
    square1, square2 = b1, b2
    for bit in range(16):
        on = ((count >> bit) & 1) == 1
        power1 = jnp.where(on, power1 * square1, power1)
        power2 = jnp.where(on, power2 * square2, power2)
        square1 = square1 * square1
        square2 = square2 * square2
    b1, b2 = b1[:1], b2[:1]
    m = b1 * first[...] + (1.0 - b1) * gradient
    v = b2 * second[...] + (1.0 - b2) * gradient * gradient
    first[...] = m
    second[...] = v
    moves[...] = (m / (1.0 - power1[:1])) / (jnp.sqrt(v / (1.0 - power2[:1])) + adam_eps)
    for k in range(0, chunk_rows, unit):
        at = aligned(place * chunk_rows + k, unit)
        first_out[k : k + unit, :] = first[pl.ds(at, unit), :]
        second_out[k : k + unit, :] = second[pl.ds(at, unit), :]
    group = LANES // rank
    down_rows = width // group
    up_rows = width // LANES
    for j in range(2):
        spread = jnp.broadcast_to(
            moves[j * down_rows : (j + 1) * down_rows, :][:, None, :], (down_rows, group, LANES)
        ).reshape(width, LANES)
        part = jnp.where(lane_is_feature(width, rank), spread, 0.0)
        pick = lane_is_rank(rank).astype(bf16)
        high = part.astype(bf16)
        rest = part - high.astype(f32)
        middle = rest.astype(bf16)
        low_part = (rest - middle.astype(f32)).astype(bf16)
        move = cdot(pick, high, 1, 1) + cdot(pick, middle, 1, 1) + cdot(pick, low_part, 1, 1)
        new_down_t[j] = down_t[j] * (1.0 - rate_first * decay_first) - rate_first * move
        base = 2 * down_rows + j * rank * up_rows
        for cb in range(up_rows):
            cols = slice(cb * LANES, (cb + 1) * LANES)
            new_up[j, :, cols] = up[j, :, cols] * (1.0 - rate_second * decay_second) - (
                rate_second * moves[pl.ds(base + cb, rank, stride=up_rows), :]
            )


def update(beta_one, beta_two, step, own, other, down_t, up, n, held, wide, low):
    n_rows = 2 * down_t.size // LANES
    chunk_rows = n_rows // wide
    smem = pl.BlockSpec(memory_space=pltpu.SMEM)
    vm = pl.BlockSpec(memory_space=VMEM)
    return pl.pallas_call(
        lambda *refs: update_kernel(*refs, n=n, held=held, wide=wide, low=low),
        out_shape=[
            sds(down_t.shape, f32),
            sds(up.shape, f32),
            sds((chunk_rows, LANES), f32),
            sds((chunk_rows, LANES), f32),
        ],
        in_specs=[smem] * 3 + [vm] * 4,
        out_specs=[vm] * 4,
        scratch_shapes=[VMEM((n_rows, LANES), f32)] * 4,
        compiler_params=pltpu.CompilerParams(vmem_limit_bytes=16 << 20),
        name="update",
    )(beta_one, beta_two, step, own, other, down_t, up)


def digit_groups(size, first):
    bits = size.bit_length() - 1
    groups = []
    at = first
    while at < bits:
        n = min(2, bits - at)
        groups.append((at, n))
        at += n
    return groups


def swap_perm(size, mask):
    return [(i, i ^ mask) for i in range(size)]


def exchange(values, axis, size, group):
    low, n = group
    return [values] + [
        lax.ppermute(values, axis, swap_perm(size, j << low)) for j in range(1, 1 << n)
    ]


def tree_sum(parts):
    while len(parts) > 1:
        parts = [parts[i] + parts[i + 1] for i in range(0, len(parts), 2)]
    return parts[0]


def in_order(parts, digit):
    parts = list(parts)
    n = len(parts).bit_length() - 1
    for bit in range(n):
        flip = (digit >> bit) & 1
        parts = [jnp.where(flip == 1, parts[i ^ (1 << bit)], parts[i]) for i in range(len(parts))]
    return parts


def per_device(
    tokens,
    cotangent,
    valid_token_length,
    query_weight_matrix,
    key_weight_matrix,
    value_weight_matrix,
    attention_output_weight,
    inner_ffn_weight,
    outer_ffn_weight,
    query_bias_vector,
    value_bias_vector,
    attention_output_bias,
    hidden_ffn_bias,
    ffn_output_bias,
    layer_norm_gains,
    layer_norm_biases,
    adapter_down_factors,
    adapter_up_factors,
    first_moment_estimate,
    second_moment_estimate,
    first_decay_factor,
    second_decay_factor,
    optimizer_step_number,
):
    dp = lax.axis_size("dp")
    wide = lax.axis_size("wide")
    place = lax.axis_index("wide")
    n_rows = 2 * adapter_down_factors.size // LANES
    chunk_rows = n_rows // wide

    down_t = jnp.swapaxes(adapter_down_factors, 1, 2)
    mixed, midg, dq, dk, dv, folded_q, folded_v, keep, send = layer(
        valid_token_length,
        tokens,
        cotangent,
        (
            query_weight_matrix,
            key_weight_matrix,
            value_weight_matrix,
            attention_output_weight,
            inner_ffn_weight,
            outer_ffn_weight,
        ),
        (
            query_bias_vector,
            value_bias_vector,
            attention_output_bias,
            hidden_ffn_bias,
            ffn_output_bias,
        ),
        layer_norm_gains,
        layer_norm_biases,
        down_t,
        adapter_up_factors,
        wide,
    )

    def token_part(prev, after, first_row, rows):
        held_back, _ = lax.optimization_barrier((midg, after))
        return token_gradient(
            prev, held_back, dq, dk, dv, folded_q, key_weight_matrix, folded_v, first_row, rows
        )

    n_tok = tokens.shape[0]
    row = lax.broadcasted_iota(jnp.int32, keep.shape, 0)
    is_up = (row >= n_rows // 4) & (row < n_rows // 2)
    scale = jnp.where(is_up, adapter_scale, 1.0)
    kept = lax.optimization_barrier(keep * scale)
    grad = kept + lax.ppermute(send, "wide", swap_perm(wide, 1)) * scale
    token_grad = token_part(None, grad, 0, n_tok // 2)
    for i, group in enumerate(digit_groups(dp, 0)):
        pieces = exchange(grad, "dp", dp, group)
        if i == 0:
            pieces, token_grad = lax.optimization_barrier((pieces, token_grad))
        grad = tree_sum(pieces)
    token_grad = token_part(token_grad, grad, n_tok // 2, n_tok // 2)

    first = first_moment_estimate.reshape(chunk_rows, LANES)
    second = second_moment_estimate.reshape(chunk_rows, LANES)
    held = 1
    rows = n_rows // 2 + 8
    groups = digit_groups(wide, 1)
    for i, (low, n) in enumerate(groups):
        pieces = exchange(jnp.concatenate([grad, first, second], axis=0), "wide", wide, (low, n))
        if i == 0:
            pieces, token_grad = lax.optimization_barrier((pieces, token_grad))
        grad = tree_sum([p[:rows] for p in pieces])
        if i + 1 < len(groups):
            block = held * chunk_rows
            pieces = in_order(pieces, place >> low)
            first = jnp.concatenate([p[rows : rows + block] for p in pieces], axis=0)
            second = jnp.concatenate([p[rows + block :] for p in pieces], axis=0)
            held *= len(pieces)
    own = jnp.concatenate([grad] + [p[rows:] for p in pieces], axis=0)
    other = lax.ppermute(own, "wide", swap_perm(wide, 1))
    low, n = groups[-1]
    updated_down_t, updated_up, updated_first, updated_second = update(
        first_decay_factor,
        second_decay_factor,
        optimizer_step_number,
        own,
        other,
        down_t,
        adapter_up_factors,
        1 << n,
        held,
        wide,
        low,
    )
    return (
        mixed,
        token_grad,
        jnp.swapaxes(updated_down_t, 1, 2),
        updated_up,
        updated_first.reshape(-1),
        updated_second.reshape(-1),
    )


def solution(mesh):
    rows = P(("dp", "wide"), None)
    placed = (rows, rows, P(("dp", "wide"))) + (P(),) * 15 + (P("wide"), P("wide")) + (P(),) * 3
    return jax.shard_map(
        per_device,
        mesh=mesh,
        in_specs=placed,
        out_specs=(rows, rows, P(), P(), P("wide"), P("wide")),
        check_vma=False,
    )
```

```python
import jax
import jax.numpy as jnp
from jax import lax
from jax.experimental import pallas as pl
from jax.experimental.pallas import tpu as pltpu
from jax.sharding import PartitionSpec as P

HEADS = 12
HEAD_DIM = 64
LEN_A = 128
LEN_B = 256
LEN_C = 512
BUCKET = 512
LANES = 128

adapter_scale = 2.0
rate_first = 0.005
rate_second = 0.08
decay_first = 0.05
decay_second = 0.01
neg_large = -1e30
norm_eps = 1e-05
adam_eps = 1e-08

f32 = jnp.float32
bf16 = jnp.bfloat16
sds = jax.ShapeDtypeStruct
VMEM = pltpu.VMEM


def cdot(left, right, left_dim, right_dim, precision=None):
    return lax.dot_general(
        left,
        right,
        (((left_dim,), (right_dim,)), ((), ())),
        precision=precision,
        preferred_element_type=f32,
    )


def low_lanes(shape):
    return lax.broadcasted_iota(jnp.int32, shape, 1) < HEAD_DIM


def head_pair_rows(pair, with_ones):
    low = low_lanes(pair.shape)
    zero = jnp.zeros_like(pair)
    first = jnp.where(low, pair, zero)
    second = jnp.where(low, zero, pair)
    if with_ones:
        one = jnp.ones_like(pair)
        first = jnp.concatenate([first, jnp.where(low, one, zero)], axis=1)
        second = jnp.concatenate([second, jnp.where(low, zero, one)], axis=1)
    return jnp.concatenate([first, second], axis=0)


def row_mean(values):
    return jnp.sum(values, axis=1, keepdims=True) * (1.0 / values.shape[1])


def lane_is_rank(rank):
    shape = (rank, LANES)
    return lax.broadcasted_iota(jnp.int32, shape, 1) % rank == lax.broadcasted_iota(
        jnp.int32, shape, 0
    )


def lane_is_feature(rows, rank):
    shape = (rows, LANES)
    return lax.broadcasted_iota(jnp.int32, shape, 0) % (LANES // rank) == (
        lax.broadcasted_iota(jnp.int32, shape, 1) // rank
    )


def flatten_pair(flat, j, spread, up):
    rank, width = up.shape
    group = LANES // rank
    down_rows = width // group
    part = jnp.where(lane_is_feature(width, rank), spread, 0.0)
    flat[j * down_rows : (j + 1) * down_rows, :] = jnp.sum(
        part.reshape(down_rows, group, LANES), axis=1
    )
    up_rows = width // LANES
    base = 2 * down_rows + j * rank * up_rows
    for cb in range(up_rows):
        flat[pl.ds(base + cb, rank, stride=up_rows), :] = up[:, cb * LANES : (cb + 1) * LANES]


def row_moves(wide, chunk_rows):
    unit = 8 if chunk_rows % 8 == 0 else 1
    for h in range(wide // 2):
        for k in range(0, chunk_rows, unit):
            yield h * chunk_rows + k, 2 * h * chunk_rows + k, unit


def aligned(row, unit):
    return pl.multiple_of(row, unit) if unit > 1 else row


def split_half(flat, out, core, wide):
    chunk_rows = flat.shape[0] // wide
    for at, row, unit in row_moves(wide, chunk_rows):
        out[at : at + unit, :] = flat[pl.ds(aligned(row + core * chunk_rows, unit), unit), :]


def layer_kernel(
    lens,
    x_hbm,
    cot_hbm,
    wq_hbm,
    wk_hbm,
    wv_hbm,
    wo_hbm,
    w1_hbm,
    w2_hbm,
    bq,
    bv,
    bo,
    b1,
    b2,
    gains,
    shifts,
    down_t,
    up,
    mixed_hbm,
    midg_hbm,
    dq_hbm,
    dk_hbm,
    dv_hbm,
    wq_out,
    wv_out,
    keep_out,
    send_out,
    x,
    cot,
    wq,
    wk,
    wv,
    wo,
    w1,
    w2,
    acat,
    brep_q,
    brep_v,
    rowv,
    qs,
    ks,
    vs,
    dn,
    probs,
    ctx,
    inv_l,
    dctx,
    act,
    slope,
    mixed,
    midg,
    dq,
    dk,
    dv,
    g_down,
    g_up_q,
    g_up_v,
    flat,
    in_sem,
    w_sem,
    out_sem,
    *,
    wide,
):
    d_model = x.shape[1]
    n_bucket = x.shape[0] // BUCKET
    n_pair = d_model // LANES
    ff = w1.shape[1]
    rank = up.shape[1]
    core = lax.rem(lax.axis_index("wide"), 2)

    def bucket_copy(i, src, dst, sem):
        rows = pl.ds(i * BUCKET, BUCKET)
        return pltpu.make_async_copy(src.at[rows, :], dst.at[rows, :], sem)

    weights = [(wq_hbm, wq), (wk_hbm, wk), (wv_hbm, wv), (wo_hbm, wo), (w1_hbm, w1), (w2_hbm, w2)]
    weight_copies = [pltpu.make_async_copy(s, d, w_sem.at[i]) for i, (s, d) in enumerate(weights)]
    x_copies = [bucket_copy(i, x_hbm, x, in_sem.at[i]) for i in range(n_bucket)]
    cot_copies = [bucket_copy(i, cot_hbm, cot, in_sem.at[n_bucket + i]) for i in range(n_bucket)]
    x_copies[-1].start()
    for i in (0, 2, 1, 3):
        weight_copies[i].start()
    cot_copies[-1].start()
    for c in weight_copies[4:]:
        c.start()
    for i in reversed(range(n_bucket - 1)):
        x_copies[i].start()
        cot_copies[i].start()

    acat[...] = jnp.concatenate(
        [down_t[0], down_t[1], jnp.zeros((LANES - 2 * rank, d_model), f32)], axis=0
    ).astype(bf16)
    up_q = up[0].astype(bf16).astype(f32) * adapter_scale
    up_v = up[1].astype(bf16).astype(f32) * adapter_scale
    brep_q[...] = jnp.concatenate([up_q] * (LANES // rank), axis=0).astype(bf16)
    brep_v[...] = jnp.concatenate([up_v] * (LANES // rank), axis=0).astype(bf16)
    seq = 0
    row0 = 0
    n_valid = 0
    for length in (LEN_A, LEN_B, LEN_C):
        for s in range(BUCKET // length):
            n = lens[seq]
            n_valid = n_valid + n
            rowv[row0 : row0 + length, :] = (
                lax.broadcasted_iota(jnp.int32, (length, LANES), 0) < n
            ).astype(f32)
            seq += 1
            row0 += length
    g_down[...] = jnp.zeros_like(g_down)
    g_up_q[...] = jnp.zeros_like(g_up_q)
    g_up_v[...] = jnp.zeros_like(g_up_v)

    def pair_at(p, row):
        if isinstance(p, int):
            return slice(p * LANES, (p + 1) * LANES), p * BUCKET + row
        return (
            pl.ds(pl.multiple_of(p * LANES, LANES), LANES),
            pl.multiple_of(p * BUCKET + row, LANES),
        )

    def each_pair(per_step, body):
        if per_step == n_pair:
            for p in range(n_pair):
                body(p, p)
            return

        def step_of(i, carry):
            for j in range(per_step):
                body(i * per_step + j, j)
            return carry

        lax.fori_loop(0, n_pair // per_step, step_of, 0)

    def attend(length, first_seq, p, s):
        rows = slice(s * length, (s + 1) * length)
        cols, prow = pair_at(p, s * length)
        key_rows = head_pair_rows(ks[rows, cols], False)
        val_rows = head_pair_rows(vs[rows, cols], True)
        lane = lax.broadcasted_iota(jnp.int32, (1, length), 1)
        bias = jnp.where(lane < lens[first_seq + s], 0.0, neg_large).astype(f32)
        scores = cdot(qs[rows, cols], key_rows, 1, 1)
        parts = []
        for h in range(2):
            sh = scores[:, h * length : (h + 1) * length] + bias
            parts.append(jnp.exp(sh - jnp.max(sh, axis=1, keepdims=True)).astype(bf16))
        e = jnp.concatenate(parts, axis=1)
        probs[pl.ds(prow, length), : 2 * length] = e
        out = cdot(e, val_rows, 1, 0)
        inv = 1.0 / out[:, LANES:]
        inv_l[rows, cols] = inv
        ctx[rows, cols] = (out[:, :LANES] * inv).astype(bf16)

    def attend_back(length, p, s, values_first):
        rows = slice(s * length, (s + 1) * length)
        cols, prow = pair_at(p, s * length)
        key_rows = head_pair_rows(ks[rows, cols], False)
        val_rows = head_pair_rows(vs[rows, cols], True)
        low = low_lanes((length, LANES))
        dcf = dctx[rows, cols].astype(f32) * inv_l[rows, cols]
        dc = dcf.astype(bf16)
        inner = (-dcf * ctx[rows, cols].astype(f32)).astype(bf16)
        e = probs[pl.ds(prow, length), : 2 * length]

        def value_part():
            rv = cdot(e, dc, 0, 0)
            dv[rows, cols] = jnp.where(low, rv[:length], rv[length:]).astype(bf16)

        if values_first:
            value_part()
        g = cdot(jnp.concatenate([dc, inner], axis=1), val_rows, 1, 1)
        ds = (e.astype(f32) * g).astype(bf16)
        dq[rows, cols] = (cdot(ds, key_rows, 1, 0) * (HEAD_DIM**-0.5)).astype(bf16)
        rk = cdot(ds, qs[rows, cols], 0, 0)
        dk[rows, cols] = jnp.where(low, rk[:length], rk[length:]).astype(bf16)
        if not values_first:
            value_part()

    size = BUCKET // 2
    ahead = (6, 6, 6)
    back = (6, 3, 3)
    step = 256

    def chain(b):
        lrows = [slice(c * size, (c + 1) * size) for c in range(2)]
        grows = [pl.ds(pl.multiple_of(b * BUCKET + c * size, size), size) for c in range(2)]

        def first_norm(c):
            ms = cdot(ctx[lrows[c], :], wo[...], 1, 0) + bo[...][None] + x[grows[c], :].astype(f32)
            xc = ms - row_mean(ms)
            r1 = lax.rsqrt(row_mean(xc * xc) + norm_eps)
            n1 = xc * r1
            return r1, n1, n1 * gains[0:1, :] + shifts[0:1, :]

        def inner_ffn(c, nl):
            for n in range(0, ff, step):
                h = cdot(nl, w1[:, n : n + step], 1, 0) + b1[n : n + step][None]
                cdf = 0.5 + 0.5 * lax.erf(h * (0.5**0.5))
                pdf = jnp.exp(h * h * -0.5) * 0.3989422804014327
                act[lrows[c], n : n + step] = (h * cdf).astype(bf16)
                slope[lrows[c], n : n + step] = (cdf + h * pdf).astype(bf16)

        def second_norm(c, normed):
            fs = cdot(act[lrows[c], :], w2[...], 1, 0) + b2[...][None] + normed
            fc = fs - row_mean(fs)
            r2 = lax.rsqrt(row_mean(fc * fc) + norm_eps)
            n2 = fc * r2
            mixed[lrows[c], :] = (n2 * gains[1:2, :] + shifts[1:2, :]).astype(bf16)
            rv = rowv[grows[c], :]
            e2 = cot[grows[c], :].astype(f32) * jnp.concatenate([rv] * n_pair, axis=1)
            e2 = e2 * gains[1:2, :]
            return r2 * (e2 - row_mean(e2) - n2 * row_mean(e2 * n2))

        def inner_back(c, ol):
            for n in range(0, ff, step):
                da = cdot(ol, w2[n : n + step, :], 1, 1).astype(bf16)
                act[lrows[c], n : n + step] = da * slope[lrows[c], n : n + step]

        def first_back(c, fg, r1, n1):
            e1 = (fg + cdot(act[lrows[c], :], w1[...], 1, 1)) * gains[0:1, :]
            mg = r1 * (e1 - row_mean(e1) - n1 * row_mean(e1 * n1))
            low = mg.astype(bf16)
            midg[lrows[c], :] = low
            dctx[lrows[c], :] = cdot(low, wo[...], 1, 1).astype(bf16)

        r1_a, n1_a, normed_a = first_norm(0)
        r1_b, n1_b, normed_b = first_norm(1)
        inner_ffn(0, normed_a.astype(bf16))
        grad_a = second_norm(0, normed_a)
        inner_ffn(1, normed_b.astype(bf16))
        inner_back(0, grad_a.astype(bf16))
        grad_b = second_norm(1, normed_b)
        first_back(0, grad_a, r1_a, n1_a)
        inner_back(1, grad_b.astype(bf16))
        first_back(1, grad_b, r1_b, n1_b)

    outs = [(mixed, mixed_hbm), (midg, midg_hbm), (dq, dq_hbm), (dk, dk_hbm), (dv, dv_hbm)]
    folded = [(wq, wq_out), (wv, wv_out)]
    folded_copies = [
        pltpu.make_async_copy(s, d, out_sem.at[len(outs) + i]) for i, (s, d) in enumerate(folded)
    ]

    def out_copy(i, b):
        rows = pl.ds(pl.multiple_of(b * BUCKET, BUCKET), BUCKET)
        src, dst = outs[i]
        return pltpu.make_async_copy(src, dst.at[rows, :], out_sem.at[i])

    def out_free(which, b):
        if b < n_bucket - 1:
            for i in which:
                out_copy(i, b + 1).wait()

    for i, w, low, high in ((0, wq, down_t[0], up_q), (2, wv, down_t[1], up_v)):
        weight_copies[i].wait()
        w[...] = (
            w[...].astype(f32) + cdot(low.astype(bf16), high.astype(bf16), 0, 0)
        ).astype(bf16)
    weight_copies[1].wait()
    for c in folded_copies:
        c.start()

    def bucket(step_b, carry):
        b = n_bucket - 1 - step_b
        rows = pl.ds(pl.multiple_of(b * BUCKET, BUCKET), BUCKET)

        def wait_bucket(src, dst, base):
            pltpu.make_async_copy(src.at[rows, :], dst.at[rows, :], in_sem.at[base + b]).wait()

        wait_bucket(x_hbm, x, 0)

        xb = x[rows, :]
        dnb = cdot(xb, acat[...], 1, 1).astype(bf16)
        dn[...] = dnb
        qs[...] = (cdot(xb, wq[...], 1, 0) + bq[...][None]).astype(bf16) * jnp.asarray(
            HEAD_DIM**-0.5, bf16
        )
        ks[...] = cdot(xb, wk[...], 1, 0).astype(bf16)
        vs[...] = (cdot(xb, wv[...], 1, 0) + bv[...][None]).astype(bf16)

        first = 0
        for i, length in enumerate((LEN_A, LEN_B, LEN_C)):
            count = BUCKET // length

            @pl.when(b == i)
            def _(i=i, length=length, first=first, count=count):
                def both(p, place):
                    for s in range(count):
                        attend(length, first, p, s)

                each_pair(ahead[i], both)
                wait_bucket(cot_hbm, cot, n_bucket)
                out_free((0, 1), i)
                if i == n_bucket - 1:
                    for c in weight_copies[3:]:
                        c.wait()

            first += count

        chain(b)
        for i in (0, 1):
            out_copy(i, b).start()

        for i, length in enumerate((LEN_A, LEN_B, LEN_C)):
            count = BUCKET // length

            @pl.when(b == i)
            def _(i=i, length=length, count=count):
                out_free((2, 3, 4), i)

                def both(p, place):
                    for s in range(count):
                        attend_back(length, p, s, (place * count + s) % 2 == 1)

                each_pair(back[i], both)

        for i in (2, 3, 4):
            out_copy(i, b).start()
        dqb = dq[...]
        dvb = dv[...]
        dgb = jnp.concatenate(
            [cdot(dqb, brep_q[...], 1, 1).astype(bf16), cdot(dvb, brep_v[...], 1, 1).astype(bf16)],
            axis=1,
        )
        g_down[...] += cdot(x[rows, :], dgb, 0, 0)
        dnb2 = dn[:, : 2 * rank]
        g_up_q[...] += cdot(dnb2, dqb, 0, 0)
        g_up_v[...] += cdot(dnb2, dvb, 0, 0)
        return carry

    lax.fori_loop(0, n_bucket, bucket, 0)

    for j, src in enumerate((g_up_q, g_up_v)):
        flatten_pair(
            flat,
            j,
            g_down[:, j * LANES : (j + 1) * LANES],
            src[j * rank : (j + 1) * rank, :],
        )
    n_rows = flat.shape[0]
    split_half(flat, keep_out, core, wide)
    split_half(flat, send_out, 1 - core, wide)
    total = jnp.full((8, LANES), n_valid, jnp.int32).astype(f32)
    keep_out[n_rows // 2 :, :] = total
    send_out[n_rows // 2 :, :] = total
    for i in range(len(outs)):
        out_copy(i, 0).wait()
    for c in folded_copies:
        c.wait()


def layer(lens, x, cot, ws, vecs, gains, shifts, down_t, up, wide):
    t, d = x.shape
    ff = ws[4].shape[1]
    rank = up.shape[1]
    n_rows = 2 * down_t.size // LANES
    n_bucket = t // BUCKET
    any_spec = pl.BlockSpec(memory_space=pl.ANY)
    vm = pl.BlockSpec(memory_space=VMEM)
    ops = [lens, x, cot, *ws, *vecs, gains, shifts, down_t, up]
    in_specs = (
        [pl.BlockSpec(memory_space=pltpu.SMEM)] + [any_spec] * 8 + [vm] * (len(vecs) + 4)
    )
    out_shape = [
        sds((t, d), bf16),
        sds((t, d), bf16),
        sds((t, d), bf16),
        sds((t, d), bf16),
        sds((t, d), bf16),
        sds((d, d), bf16),
        sds((d, d), bf16),
        sds((n_rows // 2 + 8, LANES), f32),
        sds((n_rows // 2 + 8, LANES), f32),
    ]
    dma = pltpu.SemaphoreType.DMA
    scratch = [
        VMEM((t, d), bf16),
        VMEM((t, d), bf16),
        VMEM((d, d), bf16),
        VMEM((d, d), bf16),
        VMEM((d, d), bf16),
        VMEM((d, d), bf16),
        VMEM((d, ff), bf16),
        VMEM((ff, d), bf16),
        VMEM((LANES, d), bf16),
        VMEM((LANES, d), bf16),
        VMEM((LANES, d), bf16),
        VMEM((t, LANES), f32),
        VMEM((BUCKET, d), bf16),
        VMEM((BUCKET, d), bf16),
        VMEM((BUCKET, d), bf16),
        VMEM((BUCKET, LANES), bf16),
        VMEM((d // LANES * BUCKET, 2 * LEN_C), bf16),
        VMEM((BUCKET, d), bf16),
        VMEM((BUCKET, d), f32),
        VMEM((BUCKET, d), bf16),
        VMEM((BUCKET, ff), bf16),
        VMEM((BUCKET, ff), bf16),
        VMEM((BUCKET, d), bf16),
        VMEM((BUCKET, d), bf16),
        VMEM((BUCKET, d), bf16),
        VMEM((BUCKET, d), bf16),
        VMEM((BUCKET, d), bf16),
        VMEM((d, 2 * LANES), f32),
        VMEM((2 * rank, d), f32),
        VMEM((2 * rank, d), f32),
        VMEM((n_rows, LANES), f32),
        dma((2 * n_bucket,)),
        dma((6,)),
        dma((7,)),
    ]
    body = lambda *refs: layer_kernel(*refs, wide=wide)
    return pl.pallas_call(
        body,
        out_shape=out_shape,
        in_specs=in_specs,
        out_specs=[any_spec] * 7 + [vm] * 2,
        scratch_shapes=scratch,
        compiler_params=pltpu.CompilerParams(vmem_limit_bytes=63 << 20),
        name="layer",
    )(*ops)


def token_kernel(*refs, first_row):
    mg_hbm, dq_hbm, dk_hbm, dv_hbm, wq_hbm, wk_hbm, wv_hbm, out_hbm = refs[-16:-8]
    mg, grads, weights, acc, out, g_sem, w_sem, m_sem = refs[-8:]
    rows = mg.shape[0]
    chunk = rows // 2
    whole = slice(first_row, first_row + rows)
    for i, (d_hbm, w_hbm) in enumerate(((dq_hbm, wq_hbm), (dk_hbm, wk_hbm), (dv_hbm, wv_hbm))):
        pltpu.make_async_copy(w_hbm, weights.at[i], w_sem.at[i]).start()
        pltpu.make_async_copy(d_hbm.at[whole, :], grads.at[i], g_sem.at[i]).start()
    mid = pltpu.make_async_copy(mg_hbm.at[whole, :], mg, m_sem.at[0])
    mid.start()

    def side(i, carry):
        pltpu.make_async_copy(wq_hbm, weights.at[i], w_sem.at[i]).wait()
        pltpu.make_async_copy(dq_hbm.at[whole, :], grads.at[i], g_sem.at[i]).wait()
        for c in range(2):
            local = slice(c * chunk, (c + 1) * chunk)
            part = cdot(grads[i, local, :], weights[i], 1, 1)
            acc[local, :] = jnp.where(i == 0, part, acc[local, :] + part)
        return carry

    whole_loop = first_row > 0
    lax.fori_loop(0, 3 if whole_loop else 2, side, 0)
    if not whole_loop:
        pltpu.make_async_copy(wq_hbm, weights.at[2], w_sem.at[2]).wait()
        pltpu.make_async_copy(dq_hbm.at[whole, :], grads.at[2], g_sem.at[2]).wait()
    mid.wait()
    writes = []
    for c in range(2):
        local = slice(c * chunk, (c + 1) * chunk)
        total = acc[local, :]
        if not whole_loop:
            total = total + cdot(grads[2, local, :], weights[2], 1, 1)
        out[local, :] = (total + mg[local, :].astype(f32)).astype(bf16)
        at = slice(first_row + c * chunk, first_row + (c + 1) * chunk)
        writes.append(
            pltpu.make_async_copy(out.at[local, :], out_hbm.at[at, :], m_sem.at[1 + c])
        )
        writes[-1].start()
    for w in writes:
        w.wait()


def token_gradient(prev, mg, dq, dk, dv, wq, wk, wv, first_row, rows):
    t, d = mg.shape
    any_spec = pl.BlockSpec(memory_space=pl.ANY)
    args = (mg, dq, dk, dv, wq, wk, wv)
    aliases = {}
    if prev is not None:
        args = (prev,) + args
        aliases = {0: 0}
    dma = pltpu.SemaphoreType.DMA
    return pl.pallas_call(
        lambda *refs: token_kernel(*refs, first_row=first_row),
        out_shape=sds((t, d), bf16),
        in_specs=[any_spec] * len(args),
        out_specs=any_spec,
        scratch_shapes=[
            VMEM((rows, d), bf16),
            VMEM((3, rows, d), bf16),
            VMEM((3, d, d), bf16),
            VMEM((rows, d), f32),
            VMEM((rows, d), bf16),
            dma((3,)),
            dma((3,)),
            dma((3,)),
        ],
        input_output_aliases=aliases,
        compiler_params=pltpu.CompilerParams(vmem_limit_bytes=60 << 20),
        cost_estimate=pl.CostEstimate(
            flops=6 * rows * d * d, bytes_accessed=10 * rows * d, transcendentals=0
        ),
        name="token_gradient",
    )(*args)


def update_kernel(
    beta_one, beta_two, step, own, other, down_t, up, new_down_t, new_up, first_out, second_out, *scratch, n, held, wide, low
):
    grads, first, second, moves = scratch
    rank, width = up.shape[1:]
    n_rows = grads.shape[0]
    rows = n_rows // 2
    chunk_rows = n_rows // wide
    place = lax.axis_index("wide")
    core = lax.rem(place, 2)
    digit = (place >> low) % n
    unit = 8 if chunk_rows % 8 == 0 else 1

    def put(dst, chunk, src, at):
        for k in range(0, chunk_rows, unit):
            row = aligned(chunk * chunk_rows + k, unit)
            dst[pl.ds(row, unit), :] = src[at + k : at + k + unit, :]

    block = held * chunk_rows
    for src, parity in ((own, core), (other, 1 - core)):
        for h in range(wide // 2):
            put(grads, 2 * h + parity, src, h * chunk_rows)
        for j in range(n):
            for i in range(held):
                chunk = 2 * ((digit ^ j) * held + i) + parity
                at = rows + 8 + 2 * j * block + i * chunk_rows
                put(first, chunk, src, at)
                put(second, chunk, src, at + block)
    gradient = grads[...] / own[rows : rows + 1, :]
    b1 = jnp.full((8, LANES), beta_one[0], f32)
    b2 = jnp.full((8, LANES), beta_two[0], f32)
    count = step[0]
    power1 = jnp.ones((8, LANES), f32)
    power2 = power1
    square1, square2 = b1, b2
    for bit in range(16):
        on = ((count >> bit) & 1) == 1
        power1 = jnp.where(on, power1 * square1, power1)
        power2 = jnp.where(on, power2 * square2, power2)
        square1 = square1 * square1
        square2 = square2 * square2
    b1, b2 = b1[:1], b2[:1]
    m = b1 * first[...] + (1.0 - b1) * gradient
    v = b2 * second[...] + (1.0 - b2) * gradient * gradient
    first[...] = m
    second[...] = v
    moves[...] = (m / (1.0 - power1[:1])) / (jnp.sqrt(v / (1.0 - power2[:1])) + adam_eps)
    for k in range(0, chunk_rows, unit):
        at = aligned(place * chunk_rows + k, unit)
        first_out[k : k + unit, :] = first[pl.ds(at, unit), :]
        second_out[k : k + unit, :] = second[pl.ds(at, unit), :]
    group = LANES // rank
    down_rows = width // group
    up_rows = width // LANES
    for j in range(2):
        spread = jnp.broadcast_to(
            moves[j * down_rows : (j + 1) * down_rows, :][:, None, :], (down_rows, group, LANES)
        ).reshape(width, LANES)
        part = jnp.where(lane_is_feature(width, rank), spread, 0.0)
        pick = lane_is_rank(rank).astype(bf16)
        high = part.astype(bf16)
        rest = part - high.astype(f32)
        middle = rest.astype(bf16)
        low_part = (rest - middle.astype(f32)).astype(bf16)
        move = cdot(pick, high, 1, 1) + cdot(pick, middle, 1, 1) + cdot(pick, low_part, 1, 1)
        new_down_t[j] = down_t[j] * (1.0 - rate_first * decay_first) - rate_first * move
        base = 2 * down_rows + j * rank * up_rows
        for cb in range(up_rows):
            cols = slice(cb * LANES, (cb + 1) * LANES)
            new_up[j, :, cols] = up[j, :, cols] * (1.0 - rate_second * decay_second) - (
                rate_second * moves[pl.ds(base + cb, rank, stride=up_rows), :]
            )


def update(beta_one, beta_two, step, own, other, down_t, up, n, held, wide, low):
    n_rows = 2 * down_t.size // LANES
    chunk_rows = n_rows // wide
    smem = pl.BlockSpec(memory_space=pltpu.SMEM)
    vm = pl.BlockSpec(memory_space=VMEM)
    return pl.pallas_call(
        lambda *refs: update_kernel(*refs, n=n, held=held, wide=wide, low=low),
        out_shape=[
            sds(down_t.shape, f32),
            sds(up.shape, f32),
            sds((chunk_rows, LANES), f32),
            sds((chunk_rows, LANES), f32),
        ],
        in_specs=[smem] * 3 + [vm] * 4,
        out_specs=[vm] * 4,
        scratch_shapes=[VMEM((n_rows, LANES), f32)] * 4,
        compiler_params=pltpu.CompilerParams(vmem_limit_bytes=16 << 20),
        name="update",
    )(beta_one, beta_two, step, own, other, down_t, up)


def digit_groups(size, first):
    bits = size.bit_length() - 1
    groups = []
    at = first
    while at < bits:
        n = min(2, bits - at)
        groups.append((at, n))
        at += n
    return groups


def swap_perm(size, mask):
    return [(i, i ^ mask) for i in range(size)]


def exchange(values, axis, size, group):
    low, n = group
    return [values] + [
        lax.ppermute(values, axis, swap_perm(size, j << low)) for j in range(1, 1 << n)
    ]


def tree_sum(parts):
    while len(parts) > 1:
        parts = [parts[i] + parts[i + 1] for i in range(0, len(parts), 2)]
    return parts[0]


def in_order(parts, digit):
    parts = list(parts)
    n = len(parts).bit_length() - 1
    for bit in range(n):
        flip = (digit >> bit) & 1
        parts = [jnp.where(flip == 1, parts[i ^ (1 << bit)], parts[i]) for i in range(len(parts))]
    return parts


def per_device(
    tokens,
    cotangent,
    valid_token_length,
    query_weight_matrix,
    key_weight_matrix,
    value_weight_matrix,
    attention_output_weight,
    inner_ffn_weight,
    outer_ffn_weight,
    query_bias_vector,
    value_bias_vector,
    attention_output_bias,
    hidden_ffn_bias,
    ffn_output_bias,
    layer_norm_gains,
    layer_norm_biases,
    adapter_down_factors,
    adapter_up_factors,
    first_moment_estimate,
    second_moment_estimate,
    first_decay_factor,
    second_decay_factor,
    optimizer_step_number,
):
    dp = lax.axis_size("dp")
    wide = lax.axis_size("wide")
    place = lax.axis_index("wide")
    n_rows = 2 * adapter_down_factors.size // LANES
    chunk_rows = n_rows // wide

    down_t = jnp.swapaxes(adapter_down_factors, 1, 2)
    mixed, midg, dq, dk, dv, folded_q, folded_v, keep, send = layer(
        valid_token_length,
        tokens,
        cotangent,
        (
            query_weight_matrix,
            key_weight_matrix,
            value_weight_matrix,
            attention_output_weight,
            inner_ffn_weight,
            outer_ffn_weight,
        ),
        (
            query_bias_vector,
            value_bias_vector,
            attention_output_bias,
            hidden_ffn_bias,
            ffn_output_bias,
        ),
        layer_norm_gains,
        layer_norm_biases,
        down_t,
        adapter_up_factors,
        wide,
    )

    def token_part(prev, after, first_row, rows):
        held_back, _ = lax.optimization_barrier((midg, after))
        return token_gradient(
            prev, held_back, dq, dk, dv, folded_q, key_weight_matrix, folded_v, first_row, rows
        )

    n_tok = tokens.shape[0]
    row = lax.broadcasted_iota(jnp.int32, keep.shape, 0)
    is_up = (row >= n_rows // 4) & (row < n_rows // 2)
    scale = jnp.where(is_up, adapter_scale, 1.0)
    kept = lax.optimization_barrier(keep * scale)
    grad = kept + lax.ppermute(send, "wide", swap_perm(wide, 1)) * scale
    token_grad = token_part(None, grad, 0, n_tok // 2)
    for i, group in enumerate(digit_groups(dp, 0)):
        pieces = exchange(grad, "dp", dp, group)
        if i == 0:
            pieces, token_grad = lax.optimization_barrier((pieces, token_grad))
        grad = tree_sum(pieces)
    token_grad = token_part(token_grad, grad, n_tok // 2, n_tok // 2)

    first = first_moment_estimate.reshape(chunk_rows, LANES)
    second = second_moment_estimate.reshape(chunk_rows, LANES)
    held = 1
    rows = n_rows // 2 + 8
    groups = digit_groups(wide, 1)
    for i, (low, n) in enumerate(groups):
        pieces = exchange(jnp.concatenate([grad, first, second], axis=0), "wide", wide, (low, n))
        if i == 0:
            pieces, token_grad = lax.optimization_barrier((pieces, token_grad))
        grad = tree_sum([p[:rows] for p in pieces])
        if i + 1 < len(groups):
            block = held * chunk_rows
            pieces = in_order(pieces, place >> low)
            first = jnp.concatenate([p[rows : rows + block] for p in pieces], axis=0)
            second = jnp.concatenate([p[rows + block :] for p in pieces], axis=0)
            held *= len(pieces)
    own = jnp.concatenate([grad] + [p[rows:] for p in pieces], axis=0)
    other = lax.ppermute(own, "wide", swap_perm(wide, 1))
    low, n = groups[-1]
    updated_down_t, updated_up, updated_first, updated_second = update(
        first_decay_factor,
        second_decay_factor,
        optimizer_step_number,
        own,
        other,
        down_t,
        adapter_up_factors,
        1 << n,
        held,
        wide,
        low,
    )
    return (
        mixed,
        token_grad,
        jnp.swapaxes(updated_down_t, 1, 2),
        updated_up,
        updated_first.reshape(-1),
        updated_second.reshape(-1),
    )


def solution(mesh):
    rows = P(("dp", "wide"), None)
    placed = (rows, rows, P(("dp", "wide"))) + (P(),) * 15 + (P("wide"), P("wide")) + (P(),) * 3
    return jax.shard_map(
        per_device,
        mesh=mesh,
        in_specs=placed,
        out_specs=(rows, rows, P(), P(), P("wide"), P("wide")),
        check_vma=False,
    )
```
